128 devices in a mesh: scen: 16 (over z_lo, y, core), col: 8 (over z_hi, x).
Axes of the slice: x: 4, y: 4, z: 4 (z_hi: 2, z_lo: 2; z = z_hi * 2 + z_lo), core: 2. Of those that a mesh axis runs over, the one named last changes fastest.
Arguments:
- private_seeds: float32 [16, 8, 2, 768, 256], P('scen', 'col'), may hold values from -6 to 6
- private_inverse: float32 [16, 8, 2, 768, 768], P('scen', 'col'), as said below
- coupling: bfloat16 [16, 2, 768, 16384], P('scen', None, None, 'col'), may hold values from -0.0390625 to 0.0390625
- shared_seed: float32 [8, 2048, 256], P('col', 'scen'), may hold values from -6 to 6
- shared_inverse: float32 [16, 8, 128, 8, 2048], P(None, None, None, 'col', 'scen')
Outputs:
- private_adjoint: float32 [16, 8, 2, 768, 256], P('scen', 'col')
- shared_adjoint: float32 [8, 2048, 256], P('col')
The draws below stay inside these ranges and needn't reach their ends.
Inputs may be any that keep to these rules, and one draw needn't show every extreme that they name: `private_inverse`: each 768 x 768 block is upper triangular.
All inputs are finite; a program needn't handle non-finite values.
Results may differ from the reference program's by a relative error of at most 0.0024.
Values sent between devices are 32-bit elements; how exact they have to be, the bound alone decides.
A program may use at most 128 MiB of HBM per device.

```python
import jax
import jax.numpy as jnp
from jax import lax

P_SIZE = 768
NSH = 16384
SEEDS = 256
BLK = 2
SHC = 2048
SUB = 128
N_SCEN = 16
N_COL = 8


def draw_private_inverse(key, part):
    shape = (N_SCEN, N_COL, BLK, P_SIZE, P_SIZE)
    first_key, second_key = jax.random.split(jax.random.fold_in(key, 11))
    spread = jax.random.normal(first_key, shape, jnp.float32) * (0.6 / P_SIZE ** 0.5)
    diagonal = jnp.exp(jax.random.uniform(second_key, shape[:-1], jnp.float32, -0.6931472, 0.6931472))
    row_index = lax.broadcasted_iota(jnp.int32, (P_SIZE, P_SIZE), 0)
    col_index = lax.broadcasted_iota(jnp.int32, (P_SIZE, P_SIZE), 1)
    upper = jnp.where(col_index > row_index, spread, 0.0)
    return upper + jnp.where(col_index == row_index, diagonal[..., None], 0.0)


def draw_shared_inverse(key, part):
    shape = (N_SCEN, N_COL, SUB, N_COL, SHC)
    first_key, second_key = jax.random.split(jax.random.fold_in(key, 23))
    spread = jax.random.normal(first_key, shape, jnp.float32) * (1.0 / NSH ** 0.5)
    diagonal = jax.random.uniform(second_key, shape, jnp.float32, 1.0, 2.0)
    row_global = lax.broadcasted_iota(jnp.int32, (N_SCEN, N_COL, SUB, 1, 1), 1) * SHC + lax.broadcasted_iota(jnp.int32, (N_SCEN, N_COL, SUB, 1, 1), 0) * SUB + lax.broadcasted_iota(jnp.int32, (N_SCEN, N_COL, SUB, 1, 1), 2)
    col_global = lax.broadcasted_iota(jnp.int32, (1, 1, 1, N_COL, SHC), 3) * SHC + lax.broadcasted_iota(jnp.int32, (1, 1, 1, N_COL, SHC), 4)
    return spread + jnp.where(row_global == col_global, diagonal, 0.0)


def level_of(own_key, dims, cuts, smallest, largest):
    gain, own = 1.0, jax.random.fold_in(own_key, 6)
    for dim, blocks in cuts:
        draws = jnp.exp(jax.random.uniform(jax.random.fold_in(own, dim), (blocks,), jnp.float32, smallest / len(cuts), largest / len(cuts)))
        gain = gain * jnp.repeat(draws, dims[dim] // blocks).reshape([-1 if axis == dim else 1 for axis in range(len(dims))])
    return gain


def normal_values(rng, extent, width, bound, cuts=(), held_as=jnp.bfloat16):
    entries = jax.random.normal(rng, extent, jnp.float32) * width
    if len(cuts) > 0:
        entries = level_of(rng, extent, cuts, -0.22, 0.18) * entries
    return jnp.clip(entries, min=-bound, max=bound).astype(held_as)


def setup_inputs(seed: int = 0) -> dict:
    splits = jax.random.split(jax.random.key(seed), 6)
    private_seeds = normal_values(splits[0], (N_SCEN, N_COL, BLK, P_SIZE, SEEDS), 1.0, 6.0, ((0, 16), (1, 8)), jnp.float32)
    private_inverse = draw_private_inverse(jax.random.fold_in(splits[5], 71), 0)
    coupling = normal_values(splits[2], (N_SCEN, BLK, P_SIZE, NSH), (P_SIZE * N_SCEN * BLK) ** -0.5, 0.0390625, ((0, 16), (3, 8)))
    shared_seed = normal_values(splits[3], (N_COL, SHC, SEEDS), 1.0, 6.0, ((0, 8), (1, 16)), jnp.float32)
    shared_inverse = draw_shared_inverse(jax.random.fold_in(splits[5], 71), 0)
    return dict(private_seeds=private_seeds, private_inverse=private_inverse, coupling=coupling, shared_seed=shared_seed, shared_inverse=shared_inverse)


def coupled_sum(pair):
    block_coupling, block_adjoint = pair
    return lax.dot_general(block_coupling, block_adjoint, (((0,), (0,)), ((), ())), preferred_element_type=jnp.float32)


def coupled_product(pair):
    block_coupling, shard_adjoint = pair
    return jnp.dot(block_coupling, shard_adjoint, preferred_element_type=jnp.float32)


def reference(private_seeds, private_inverse, coupling, shared_seed, shared_inverse):
    highest = lax.Precision.HIGHEST
    first = jnp.einsum("scbqp,scbqe->scbpe", private_inverse, private_seeds, precision=highest)
    first_half = first.astype(jnp.bfloat16)
    coupled = coupling.reshape(N_SCEN, BLK, P_SIZE, N_COL, SHC)
    coupled = jnp.moveaxis(coupled, 3, 0).reshape(N_COL, N_SCEN * BLK * P_SIZE, SHC)
    halves = jnp.moveaxis(first_half, 1, 0).reshape(N_COL, N_SCEN * BLK * P_SIZE, SEEDS)
    seed_sum = lax.map(coupled_sum, (coupled, halves))
    reduced = shared_seed - seed_sum
    applied = jnp.einsum("tkrcj,cje->ktre", shared_inverse, reduced, precision=highest)
    shared_adjoint = applied.reshape(N_COL, SHC, SEEDS)
    shared_half = shared_adjoint.astype(jnp.bfloat16)
    products = lax.map(coupled_product, (coupled, shared_half))
    products = jnp.moveaxis(products.reshape(N_COL, N_SCEN, BLK, P_SIZE, SEEDS), 0, 1)
    second = first - products
    private_adjoint = jnp.einsum("scbpq,scbqe->scbpe", private_inverse, second, precision=highest)
    return private_adjoint, shared_adjoint
```

```python
import jax
import jax.numpy as jnp
from jax import lax
from jax.experimental import pallas as pl
from jax.experimental.pallas import tpu as pltpu
from jax.sharding import PartitionSpec as P

MESH = pl.DeviceIdType.MESH
F32, BF16 = jnp.float32, jnp.bfloat16
ROWS = (48, 48, 32)
START = (0, 48, 96)
STOP = 99
MESSAGES = 160


def split(value):
    high = value.astype(BF16)
    return high, (value - high.astype(F32)).astype(BF16)


def kernel(
    seeds_h, inv_h, coup_h, sseed_h, sinv_h,
    priv_h, shared_h,
    seeds_v, inv_v, coup_v, sseed_v, part, mh0, mh1, mh2, ml0, ml1, ml2,
    inv_hi, inv_lo, half_t, sy, sz, cy, cz, ly, lz, rbuf, rcat, lr0, lr1, lr2, yg, yh,
    local_sem, send_sem, recv_sem,
):
    mhi, mlo, lands = (mh0, mh1, mh2), (ml0, ml1, ml2), (lr0, lr1, lr2)
    scen, col = lax.axis_index("scen"), lax.axis_index("col")
    core = lax.rem(scen, 2)
    y = lax.rem(lax.div(scen, 2), 4)
    zl = lax.div(scen, 8)
    x, zh = lax.rem(col, 4), lax.div(col, 4)
    z = zh * 2 + zl

    def device(x, y, z, core):
        return (lax.rem(z, 2) * 8 + y * 2 + core, lax.div(z, 2) * 4 + x)

    def ring(at, step):
        return lax.rem(at + step, 4)

    partner = device(x, y, z, 1 - core)
    zpair = ((1 - zl) * 8 + y * 2 + core, col)
    around = (
        (device(ring(x, 1), y, z, core), device(ring(x, 3), y, z, core)),
        (device(x, ring(y, 1), z, core), device(x, ring(y, 3), z, core)),
        (device(x, y, ring(z, 1), core), device(x, y, ring(z, 3), core)),
    )
    place = (x, y, z)

    loads = []

    def load(src, dst):
        copy = pltpu.make_async_copy(src, dst, local_sem.at[len(loads)])
        copy.start()
        loads.append(copy)
        return copy

    load_seeds = load(seeds_h, seeds_v)
    load_inv = [load(inv_h.at[b], inv_v.at[b]) for b in range(2)]
    load_coup = [load(coup_h.at[b], coup_v.at[b]) for b in range(2)]
    load_sseed = load(sseed_h, sseed_v)
    mine = pl.multiple_of(core * 8192, 8192)
    other = pl.multiple_of((1 - core) * 8192, 8192)
    load_sinv = load(sinv_h.at[pl.ds(mine, 8192)], part.at[pl.ds(mine, 8192)])

    barrier = pltpu.get_barrier_semaphore()
    for to in (partner, *around[0], *around[1], *around[2]):
        pl.semaphore_signal(barrier, inc=1, device_id=to, device_id_type=MESH)
    pl.semaphore_wait(barrier, 7)

    sent = []

    def send(src, dst, to):
        copy = pltpu.make_async_remote_copy(
            src_ref=src,
            dst_ref=dst,
            send_sem=send_sem.at[len(sent)],
            recv_sem=recv_sem.at[len(sent)],
            device_id=to,
            device_id_type=MESH,
        )
        copy.start()
        sent.append(copy)
        return copy

    swap_sinv = send(sinv_h.at[pl.ds(other, 8192)], part.at[pl.ds(mine, 8192)], partner)

    load_seeds.wait()
    for b in range(2):
        load_inv[b].wait()
        turned_hi, turned_lo = split(seeds_v[b].T)
        hi, lo = split(inv_v[b])
        inv_hi[b] = hi
        inv_lo[b] = lo
        for tile in range(3):
            depth, at = 256 * (tile + 1), 256 * tile
            left = jnp.concatenate(
                [turned_hi[:, :depth], turned_hi[:, :depth], turned_lo[:, :depth]], axis=1
            )
            right = jnp.concatenate(
                [
                    inv_hi[b, :depth, at : at + 256],
                    inv_lo[b, :depth, at : at + 256],
                    inv_hi[b, :depth, at : at + 256],
                ],
                axis=0,
            )
            first = jnp.dot(left, right, preferred_element_type=F32)
            half_t[:, b * 768 + at : b * 768 + at + 256] = first.astype(BF16)
            seeds_v[b, at : at + 256, :] = first.T

    for copy in load_coup:
        copy.wait()

    def seed_terms(pair, carry):
        lane = pl.multiple_of(pair * 256, 256)
        right = jnp.concatenate([coup_v[0, :, pl.ds(lane, 256)], coup_v[1, :, pl.ds(lane, 256)]], axis=0)
        terms = jnp.dot(half_t[...], right, preferred_element_type=F32)
        zl_to, y_to = lax.div(pair, 4), lax.rem(pair, 4)
        for h in range(2):
            block = terms[:, h * 128 : h * 128 + 128]
            for half in range(2):
                row = pl.multiple_of((((h * 2 + half) * 4 + y_to) * 2 + zl_to) * 64, 64)
                sy[pl.ds(row, 64), :] = block[half * 64 : half * 64 + 64]
                row = pl.multiple_of((((h * 2 + zl_to) * 2 + half) * 4 + y_to) * 64, 64)
                sz[pl.ds(row, 64), :] = block[128 + half * 64 : 192 + half * 64]
        return carry

    lax.fori_loop(0, 8, seed_terms, 0)

    def add(to, *froms):
        total = to[...]
        for ref in froms:
            total = total + ref[...]
        to[...] = total

    def ring_start(view, land, axis):
        me, (plus, minus) = place[axis], around[axis]
        p1 = send(view(0, ring(me, 2)), land(0, 0), plus)
        m1 = send(view(1, ring(me, 2)), land(1, 0), minus)
        return [p1, m1]

    def ring_second(view, land, axis):
        me, (plus, minus) = place[axis], around[axis]
        p2 = send(view(1, ring(me, 1)), land(0, 1), plus)
        m2 = send(view(0, ring(me, 3)), land(1, 1), minus)
        return [p2, m2]

    def ring_third(view, land, axis, first):
        me, (plus, minus) = place[axis], around[axis]
        first[0].wait_recv()
        add(view(0, ring(me, 1)), land(0, 0))
        p3 = send(view(0, ring(me, 1)), land(0, 2), plus)
        first[1].wait_recv()
        add(view(1, ring(me, 3)), land(1, 0))
        m3 = send(view(1, ring(me, 3)), land(1, 2), minus)
        return [p3, m3]

    def ring_own(second, third):
        for copy in (*second, *third):
            copy.wait_recv()

    send_core = pl.multiple_of((1 - core) * 1024, 1024)
    own_core = pl.multiple_of(core * 1024, 1024)
    core_z = send(sz.at[pl.ds(send_core, 1024)], cz, partner)
    core_y = send(sy.at[pl.ds(send_core, 1024)], cy, partner)

    def view_y(half, d):
        return sy.at[pl.ds(pl.multiple_of(own_core + (half * 4 + d) * 128, 128), 128)]

    def view_z(half, d):
        return sz.at[pl.ds(pl.multiple_of(own_core + ((zl * 2 + half) * 4 + d) * 64, 64), 64)]

    def land_y(way, message):
        return ly.at[pl.ds((way * 3 + message) * 128, 128)]

    def land_z(way, message):
        return lz.at[pl.ds(512 + (way * 3 + message) * 64, 64)]

    def split_shared(first, count):
        def body(block, carry):
            t, k = lax.div(block, 8), lax.rem(block, 8)
            y_to, z_to, x_to = lax.rem(t, 4), lax.div(k, 4) * 2 + lax.div(t, 4), lax.rem(k, 4)
            near = part[pl.ds(pl.multiple_of(block * 128, 128), 128), :]
            far = part[pl.ds(pl.multiple_of(8192 + block * 128, 128), 128), :]
            hi, lo = split(jnp.concatenate([near, far], axis=1))
            spots = (
                (x_to * 4 + y_to) * 4 + z_to,
                (y_to * 4 + z_to) * 4 + x_to,
                (z_to * 4 + x_to) * 4 + y_to,
            )
            for colour in range(3):
                rows, start = ROWS[colour], START[colour]
                spot = pl.multiple_of(spots[colour] * rows, rows)
                mhi[colour][pl.ds(spot, rows), :] = hi[start : start + rows]
                mlo[colour][pl.ds(spot, rows), :] = lo[start : start + rows]
            return carry

        lax.fori_loop(first, first + count, body, 0)

    core_z.wait_recv()
    add(sz.at[pl.ds(own_core, 1024)], cz)
    pair_z = send(
        sz.at[pl.ds(pl.multiple_of(own_core + (1 - zl) * 512, 512), 512)], lz.at[pl.ds(0, 512)], zpair
    )
    core_y.wait_recv()
    add(sy.at[pl.ds(own_core, 1024)], cy)
    y_first = ring_start(view_y, land_y, 1)
    y_second = ring_second(view_y, land_y, 1)
    load_sinv.wait()
    swap_sinv.wait_recv()
    split_shared(0, 16)
    y_third = ring_third(view_y, land_y, 1, y_first)
    pair_z.wait_recv()
    add(sz.at[pl.ds(pl.multiple_of(own_core + zl * 512, 512), 512)], lz.at[pl.ds(0, 512)])
    z_first = ring_start(view_z, land_z, 1)
    z_second = ring_second(view_z, land_z, 1)
    split_shared(16, 16)
    ring_own(y_second, y_third)
    add(view_y(0, y), land_y(1, 1), land_y(0, 2))
    add(view_y(1, y), land_y(0, 1), land_y(1, 2))
    pair_y = []
    for half in range(2):
        row = pl.multiple_of(own_core + ((half * 4 + y) * 2 + 1 - zl) * 64, 64)
        pair_y.append(send(sy.at[pl.ds(row, 64)], ly.at[pl.ds(768 + half * 64, 64)], zpair))
    z_third = ring_third(view_z, land_z, 1, z_first)
    split_shared(32, 32)
    pieces = []
    for half in range(2):
        pair_y[half].wait_recv()
        row = pl.multiple_of(own_core + ((half * 4 + y) * 2 + zl) * 64, 64)
        pieces.append(sy[pl.ds(row, 64), :] + ly[pl.ds(768 + half * 64, 64), :])
    ring_own(z_second, z_third)
    pieces.append(view_z(0, y)[...] + land_z(1, 1)[...] + land_z(0, 2)[...])
    pieces.append(view_z(1, y)[...] + land_z(0, 1)[...] + land_z(1, 2)[...])
    load_sseed.wait()
    rbuf[core] = sseed_v[...] - jnp.concatenate(pieces, axis=0).T
    swap_r = send(rbuf.at[core], rbuf.at[core], partner)
    swap_r.wait_recv()
    r_hi, r_lo = split(jnp.concatenate([rbuf[0], rbuf[1]], axis=0))
    rcat[0:256] = r_hi
    rcat[256:512] = r_hi
    rcat[512:768] = r_lo

    def terms(colour, d):
        rows = ROWS[colour]
        base = 128 * START[colour]

        def body(j, carry):
            row = pl.multiple_of((d * 4 + j) * 4 * rows, 4 * rows)
            high = mhi[colour][pl.ds(row, 4 * rows), :]
            left = jnp.concatenate([high, mlo[colour][pl.ds(row, 4 * rows), :], high], axis=1)
            out = jnp.dot(left, rcat[...], preferred_element_type=F32)
            part[pl.ds(pl.multiple_of(base + row, rows), 4 * rows), :] = out[:, :128]
            part[pl.ds(pl.multiple_of(base + 64 * rows + row, rows), 4 * rows), :] = out[:, 128:]
            return carry

        lax.fori_loop(0, 4, body, 0)

    order = ((0, 1, 2), (1, 2, 0), (2, 0, 1))

    def views(colour, stage):
        rows = ROWS[colour]
        axes = order[colour]
        size = (16, 4, 1)[stage] * rows
        base = 128 * START[colour]
        for step in range(stage):
            base = base + place[axes[step]] * ((16, 4)[step] * rows)

        def view(half, d):
            return part.at[pl.ds(pl.multiple_of(base + half * (64 * rows) + d * size, 16), size)]

        shift = (0, 16, 20)[stage] * rows

        def land(way, message):
            return lands[colour].at[pl.ds((way * 3 + message) * 21 * rows + shift, size)]

        return view, land, axes[stage]

    first, second, third = [None] * 3, [None] * 3, [None] * 3
    for colour in range(3):
        view, land, axis = views(colour, 0)
        terms(colour, ring(place[axis], 2))
        first[colour] = ring_start(view, land, axis)
    for colour in range(3):
        view, land, axis = views(colour, 0)
        terms(colour, ring(place[axis], 1))
        terms(colour, ring(place[axis], 3))
        second[colour] = ring_second(view, land, axis)
    for colour in range(3):
        view, land, axis = views(colour, 0)
        terms(colour, place[axis])
    block = core * 8 + zl * 4 + y
    for stage in range(3):
        for colour in range(3):
            view, land, axis = views(colour, stage)
            third[colour] = ring_third(view, land, axis, first[colour])
        for colour in range(3):
            view, land, axis = views(colour, stage)
            ring_own(second[colour], third[colour])
            if stage < 2:
                add(view(0, place[axis]), land(1, 1), land(0, 2))
                add(view(1, place[axis]), land(0, 1), land(1, 2))
                view, land, axis = views(colour, stage + 1)
                first[colour] = ring_start(view, land, axis)
                second[colour] = ring_second(view, land, axis)
            else:
                start, rows = START[colour], ROWS[colour]
                me = place[axis]
                yg[block, 0, start : start + rows] = view(0, me)[...] + land(1, 1)[...] + land(0, 2)[...]
                yg[block, 1, start : start + rows] = view(1, me)[...] + land(0, 1)[...] + land(1, 2)[...]

    yp, ym = around[1]

    def at(zl_of, y_of, half, start=0, rows=128):
        return yg.at[core * 8 + zl_of * 4 + y_of, half, start : start + rows]

    def pass_on(ref, to):
        return send(ref, ref, to)

    back, ahead, across, away = ring(y, 3), ring(y, 1), ring(y, 2), 1 - zl
    z0 = pass_on(at(zl, y, 0), zpair)
    y0 = [pass_on(at(zl, y, 0), yp), pass_on(at(zl, y, 0), ym)]
    y1 = [pass_on(at(zl, y, 1), yp), pass_on(at(zl, y, 1), ym)]
    z1 = [pass_on(at(zl, y, 1), zpair)]
    to_core = [pass_on(at(zl, y, half), partner) for half in range(2)]
    z0.wait_recv()
    y0z = [pass_on(at(away, y, 0), yp), pass_on(at(away, y, 0), ym)]
    to_core.append(pass_on(at(away, y, 0), partner))
    y1[0].wait_recv()
    y1f = [pass_on(at(zl, back, 1, 0, 64), yp)]
    z1.append(pass_on(at(zl, back, 1), zpair))
    y1[1].wait_recv()
    y1f.append(pass_on(at(zl, ahead, 1, 64, 64), ym))
    z1.append(pass_on(at(zl, ahead, 1), zpair))
    y0[0].wait_recv()
    y0f = [pass_on(at(zl, back, 0, 0, 64), yp)]
    y0[1].wait_recv()
    y0f.append(pass_on(at(zl, ahead, 0, 64, 64), ym))
    for half in (1, 0):
        to_core.append(pass_on(at(zl, back, half), partner))
        to_core.append(pass_on(at(zl, ahead, half), partner))
    y0z[0].wait_recv()
    y0zf = [pass_on(at(away, back, 0, 0, 64), yp)]
    y0z[1].wait_recv()
    y0zf.append(pass_on(at(away, ahead, 0, 64, 64), ym))
    to_core.append(pass_on(at(away, back, 0), partner))
    to_core.append(pass_on(at(away, ahead, 0), partner))
    for copy in y1f:
        copy.wait_recv()
    z1.append(pass_on(at(zl, across, 1), zpair))
    to_core.append(pass_on(at(zl, across, 1), partner))
    for copy in y0f:
        copy.wait_recv()
    to_core.append(pass_on(at(zl, across, 0), partner))
    for copy, y_of in zip(z1, (y, back, ahead, across)):
        copy.wait_recv()
        to_core.append(pass_on(at(away, y_of, 1), partner))
    for copy in y0zf:
        copy.wait_recv()
    to_core.append(pass_on(at(away, across, 0), partner))
    for copy in to_core:
        copy.wait_recv()

    store_shared = [
        load(yg.at[:, half], shared_h.at[:, :, half * 128 : half * 128 + 128]) for half in range(2)
    ]

    def round_block(t, carry):
        row = pl.multiple_of(t * 128, 128)
        yh[pl.ds(row, 128), :] = jnp.concatenate([yg[t, 0], yg[t, 1]], axis=1).astype(BF16)
        return carry

    lax.fori_loop(0, 16, round_block, 0)

    stores = []
    for b in range(2):

        def coupled(tile, carry, b=b):
            row = pl.multiple_of(tile * 256, 256)
            product = jnp.dot(coup_v[b, pl.ds(row, 256), :], yh[...], preferred_element_type=F32)
            seeds_v[b, pl.ds(row, 256), :] = seeds_v[b, pl.ds(row, 256), :] - product
            return carry

        lax.fori_loop(0, 3, coupled, 0)
        second_hi, second_lo = split(seeds_v[b])
        for tile in range(3):
            at_row = 256 * tile
            high = inv_hi[b, at_row : at_row + 256, at_row:]
            left = jnp.concatenate([high, inv_lo[b, at_row : at_row + 256, at_row:], high], axis=1)
            right = jnp.concatenate([second_hi[at_row:], second_hi[at_row:], second_lo[at_row:]], axis=0)
            inv_v[b, at_row : at_row + 256, 0:256] = jnp.dot(left, right, preferred_element_type=F32)
        stores.append(load(inv_v.at[b, :, 0:256], priv_h.at[b]))
    for copy in (*stores, *store_shared):
        copy.wait()
    for copy in sent:
        copy.wait_send()


def on_device(private_seeds, private_inverse, coupling, shared_seed, shared_inverse):
    vmem = pltpu.VMEM
    priv, shared = pl.pallas_call(
        kernel,
        out_shape=(
            jax.ShapeDtypeStruct((2, 768, 256), F32),
            jax.ShapeDtypeStruct((16, 128, 256), F32),
        ),
        in_specs=[pl.BlockSpec(memory_space=pl.ANY)] * 5,
        out_specs=[pl.BlockSpec(memory_space=pl.ANY)] * 2,
        scratch_shapes=[
            vmem((2, 768, 256), F32),
            vmem((2, 768, 768), F32),
            vmem((2, 768, 2048), BF16),
            vmem((128, 256), F32),
            vmem((16384, 128), F32),
            *[vmem((64 * rows, 256), BF16) for rows in ROWS],
            *[vmem((64 * rows, 256), BF16) for rows in ROWS],
            vmem((2, 768, 768), BF16),
            vmem((2, 768, 768), BF16),
            vmem((256, 1536), BF16),
            vmem((2048, 128), F32),
            vmem((2048, 128), F32),
            vmem((1024, 128), F32),
            vmem((1024, 128), F32),
            vmem((896, 128), F32),
            vmem((896, 128), F32),
            vmem((2, 128, 256), F32),
            vmem((768, 256), BF16),
            *[vmem((126 * rows, 128), F32) for rows in ROWS],
            vmem((16, 2, 128, 128), F32),
            vmem((2048, 256), BF16),
            pltpu.SemaphoreType.DMA((16,)),
            pltpu.SemaphoreType.DMA((MESSAGES,)),
            pltpu.SemaphoreType.DMA((MESSAGES,)),
        ],
        compiler_params=pltpu.CompilerParams(
            collective_id=0, has_side_effects=True, vmem_limit_bytes=67_043_328
        ),
        name="adjoint",
    )(
        private_seeds[0, 0],
        private_inverse[0, 0],
        coupling[0],
        shared_seed[0],
        shared_inverse.reshape(16384, 128),
    )
    return priv[None, None], shared.reshape(1, 2048, 256)


def solution(mesh):
    return jax.shard_map(
        on_device,
        mesh=mesh,
        in_specs=(
            P("scen", "col", None, None, None),
            P("scen", "col", None, None, None),
            P("scen", None, None, "col"),
            P("col", "scen", None),
            P(None, None, None, "col", "scen"),
        ),
        out_specs=(P("scen", "col", None, None, None), P("col", None, None)),
        check_vma=False,
    )
```

```python
import jax
import jax.numpy as jnp
from jax import lax
from jax.experimental import pallas as pl
from jax.experimental.pallas import tpu as pltpu
from jax.sharding import PartitionSpec as P

MESH = pl.DeviceIdType.MESH
F32, BF16 = jnp.float32, jnp.bfloat16
ROWS = (48, 48, 32)
START = (0, 48, 96)
ORDER = ((0, 2, 1), (1, 0, 2), (2, 1, 0))
SY, SZ = 80, 48
MESSAGES = 200


def split(value):
    high = value.astype(BF16)
    return high, (value - high.astype(F32)).astype(BF16)


def kernel(
    seeds_h, inv_h, coup_h, sseed_h, sinv_h,
    priv_h, shared_h,
    seeds_v, inv_v, coup_v, sseed_v, part, mh0, mh1, mh2, ml0, ml1, ml2,
    inv_hi, inv_lo, half_t, sy, sz, cy, cz, ly, lz, py, pz, rbuf, rcat, lr0, lr1, lr2, yg, yh,
    local_sem, send_sem, recv_sem,
):
    mhi, mlo, lands = (mh0, mh1, mh2), (ml0, ml1, ml2), (lr0, lr1, lr2)
    scen, col = lax.axis_index("scen"), lax.axis_index("col")
    core = lax.rem(scen, 2)
    y = lax.rem(lax.div(scen, 2), 4)
    zl = lax.div(scen, 8)
    x, zh = lax.rem(col, 4), lax.div(col, 4)
    z = zh * 2 + zl

    def device(x, y, z, core):
        return (lax.rem(z, 2) * 8 + y * 2 + core, lax.div(z, 2) * 4 + x)

    def ring(at, step):
        return lax.rem(at + step, 4)

    partner = device(x, y, z, 1 - core)
    zpair = ((1 - zl) * 8 + y * 2 + core, col)
    around = (
        (device(ring(x, 1), y, z, core), device(ring(x, 3), y, z, core)),
        (device(x, ring(y, 1), z, core), device(x, ring(y, 3), z, core)),
        (device(x, y, ring(z, 1), core), device(x, y, ring(z, 3), core)),
    )
    across = (device(ring(x, 2), y, z, core), device(x, ring(y, 2), z, core), device(x, y, ring(z, 2), core))
    place = (x, y, z)

    loads = []

    def load(src, dst):
        copy = pltpu.make_async_copy(src, dst, local_sem.at[len(loads)])
        copy.start()
        loads.append(copy)
        return copy

    load_seeds = load(seeds_h, seeds_v)
    load_inv = [load(inv_h.at[b], inv_v.at[b]) for b in range(2)]
    load_coup = [load(coup_h.at[b], coup_v.at[b]) for b in range(2)]
    load_sseed = load(sseed_h, sseed_v)
    mine = pl.multiple_of(core * 8192, 8192)
    other = pl.multiple_of((1 - core) * 8192, 8192)
    load_sinv = load(sinv_h.at[pl.ds(mine, 8192)], part.at[pl.ds(mine, 8192)])

    barrier = pltpu.get_barrier_semaphore()
    for to in (partner, *around[0], *around[1], *around[2], *across):
        pl.semaphore_signal(barrier, inc=1, device_id=to, device_id_type=MESH)

    sent = []

    def send(src, dst, to):
        copy = pltpu.make_async_remote_copy(
            src_ref=src,
            dst_ref=dst,
            send_sem=send_sem.at[len(sent)],
            recv_sem=recv_sem.at[len(sent)],
            device_id=to,
            device_id_type=MESH,
        )
        copy.start()
        sent.append(copy)
        return copy

    def swap_shared(half):
        return send(
            sinv_h.at[pl.ds(pl.multiple_of(other + half * 4096, 4096), 4096)],
            part.at[pl.ds(pl.multiple_of(mine + half * 4096, 4096), 4096)],
            partner,
        )


    load_seeds.wait()
    for b in range(2):
        load_inv[b].wait()
        turned_hi, turned_lo = split(seeds_v[b].T)
        hi, lo = split(inv_v[b])
        inv_hi[b] = hi
        inv_lo[b] = lo
        for tile in range(3):
            depth, at = 256 * (tile + 1), 256 * tile
            left = jnp.concatenate(
                [turned_hi[:, :depth], turned_hi[:, :depth], turned_lo[:, :depth]], axis=1
            )
            right = jnp.concatenate(
                [
                    inv_hi[b, :depth, at : at + 256],
                    inv_lo[b, :depth, at : at + 256],
                    inv_hi[b, :depth, at : at + 256],
                ],
                axis=0,
            )
            first = jnp.dot(left, right, preferred_element_type=F32)
            half_t[:, b * 768 + at : b * 768 + at + 256] = first.astype(BF16)
            seeds_v[b, at : at + 256, :] = first.T

    for copy in load_coup:
        copy.wait()

    def seed_terms(zl_to):
        def body(y_to, carry):
            lane = pl.multiple_of((zl_to * 4 + y_to) * 256, 256)
            right = jnp.concatenate([coup_v[0, :, pl.ds(lane, 256)], coup_v[1, :, pl.ds(lane, 256)]], axis=0)
            out = jnp.dot(half_t[...], right, preferred_element_type=F32)
            for h in range(2):
                block = out[:, h * 128 : h * 128 + 128]
                for half in range(2):
                    sy[h, zl_to, half, y_to] = block[half * SY : half * SY + SY]
                    sz[h, zl_to, half, y_to] = block[2 * SY + half * SZ : 2 * SY + half * SZ + SZ]
            return carry

        lax.fori_loop(0, 4, body, 0)

    def add(to, *froms):
        total = to[...]
        for ref in froms:
            total = total + ref[...]
        to[...] = total

    def ring_start(view, land, axis):
        me, (plus, minus) = place[axis], around[axis]
        p1 = send(view(0, ring(me, 2)), land(0, 0), plus)
        m1 = send(view(1, ring(me, 2)), land(1, 0), minus)
        return [p1, m1]

    def ring_second(view, land, axis):
        me, (plus, minus) = place[axis], around[axis]
        p2 = send(view(1, ring(me, 1)), land(0, 1), plus)
        m2 = send(view(0, ring(me, 3)), land(1, 1), minus)
        return [p2, m2]

    def ring_third(view, land, axis, first):
        me, (plus, minus) = place[axis], around[axis]
        first[0].wait_recv()
        add(view(0, ring(me, 1)), land(0, 0))
        p3 = send(view(0, ring(me, 1)), land(0, 2), plus)
        first[1].wait_recv()
        add(view(1, ring(me, 3)), land(1, 0))
        m3 = send(view(1, ring(me, 3)), land(1, 2), minus)
        return [p3, m3]

    def ring_own(second, third):
        for copy in (*second, *third):
            copy.wait_recv()

    away = 1 - zl
    core_y, core_z = [], []
    for zl_to in (away, zl):
        seed_terms(zl_to)
        if not sent:
            pl.semaphore_wait(barrier, 10)
        core_z.append(send(sz.at[1 - core, zl_to], cz.at[zl_to], partner))
        core_y.append(send(sy.at[1 - core, zl_to], cy.at[zl_to], partner))
    swaps = [swap_shared(half) for half in range(2)]

    def view_y(half, d):
        return sy.at[core, :, half, d]

    def view_z(half, d):
        return sz.at[core, zl, half, d]

    def land_y(way, message):
        return ly.at[way, message]

    def land_z(way, message):
        return lz.at[way, message]

    def split_shared(first, count):
        def body(block, carry):
            t, shard = lax.div(block, 8), lax.rem(block, 8)
            y_to, z_to, x_to = lax.rem(t, 4), lax.div(shard, 4) * 2 + lax.div(t, 4), lax.rem(shard, 4)
            near = part[pl.ds(pl.multiple_of(block * 128, 128), 128), :]
            far = part[pl.ds(pl.multiple_of(8192 + block * 128, 128), 128), :]
            hi, lo = split(jnp.concatenate([near, far], axis=1))
            to = (x_to, y_to, z_to)
            for colour in range(3):
                rows, start = ROWS[colour], START[colour]
                i, j, k = ORDER[colour]
                spot = pl.multiple_of(((to[i] * 4 + to[j]) * 4 + to[k]) * rows, rows)
                mhi[colour][pl.ds(spot, rows), :] = hi[start : start + rows]
                mlo[colour][pl.ds(spot, rows), :] = lo[start : start + rows]
            return carry

        lax.fori_loop(first, first + count, body, 0)

    core_z[0].wait_recv()
    add(sz.at[core, away], cz.at[away])
    pair_z = send(sz.at[core, away], pz, zpair)
    core_y[0].wait_recv()
    add(sy.at[core, away], cy.at[away])
    core_z[1].wait_recv()
    core_y[1].wait_recv()
    add(sy.at[core, zl], cy.at[zl])
    y_first = ring_start(view_y, land_y, 1)
    y_second = ring_second(view_y, land_y, 1)
    add(sz.at[core, zl], cz.at[zl])
    y_third = ring_third(view_y, land_y, 1, y_first)
    pair_z.wait_recv()
    add(sz.at[core, zl], pz)
    z_first = ring_start(view_z, land_z, 1)
    z_second = ring_second(view_z, land_z, 1)
    load_sinv.wait()
    swaps[0].wait_recv()
    split_shared(0, 32)
    ring_own(y_second, y_third)
    add(view_y(0, y), land_y(1, 1), land_y(0, 2))
    add(view_y(1, y), land_y(0, 1), land_y(1, 2))
    pair_y = [send(sy.at[core, away, half, y], py.at[half], zpair) for half in range(2)]
    z_third = ring_third(view_z, land_z, 1, z_first)
    swaps[1].wait_recv()
    split_shared(32, 32)
    pieces = []
    for half in range(2):
        pair_y[half].wait_recv()
        pieces.append(sy[core, zl, half, y] + py[half])
    ring_own(z_second, z_third)
    pieces.append(view_z(0, y)[...] + land_z(1, 1)[...] + land_z(0, 2)[...])
    pieces.append(view_z(1, y)[...] + land_z(0, 1)[...] + land_z(1, 2)[...])
    load_sseed.wait()
    rbuf[core] = sseed_v[...] - jnp.concatenate(pieces, axis=0).T
    swap_r = send(rbuf.at[core], rbuf.at[core], partner)
    swap_r.wait_recv()
    r_hi, r_lo = split(jnp.concatenate([rbuf[0], rbuf[1]], axis=0))
    rcat[0:256] = r_hi
    rcat[256:512] = r_hi
    rcat[512:768] = r_lo

    def terms(colour, d):
        rows = ROWS[colour]
        base = 128 * START[colour]

        def body(j, carry):
            row = pl.multiple_of((d * 4 + j) * 4 * rows, 4 * rows)
            high = mhi[colour][pl.ds(row, 4 * rows), :]
            left = jnp.concatenate([high, mlo[colour][pl.ds(row, 4 * rows), :], high], axis=1)
            out = jnp.dot(left, rcat[...], preferred_element_type=F32)
            part[pl.ds(pl.multiple_of(base + row, rows), 4 * rows), :] = out[:, :128]
            part[pl.ds(pl.multiple_of(base + 64 * rows + row, rows), 4 * rows), :] = out[:, 128:]
            return carry

        lax.fori_loop(0, 4, body, 0)

    def views(colour, stage):
        rows = ROWS[colour]
        axes = ORDER[colour]
        size = (16, 4, 1)[stage] * rows
        base = 128 * START[colour]
        for step in range(stage):
            base = base + place[axes[step]] * ((16, 4)[step] * rows)

        def view(half, d):
            return part.at[pl.ds(pl.multiple_of(base + half * (64 * rows) + d * size, 16), size)]

        shift = (0, 16, 20)[stage] * rows

        def land(way, message):
            return lands[colour].at[pl.ds((way * 3 + message) * 21 * rows + shift, size)]

        return view, land, axes[stage]

    first, second, third = [None] * 3, [None] * 3, [None] * 3
    for colour in range(3):
        view, land, axis = views(colour, 0)
        terms(colour, ring(place[axis], 2))
        first[colour] = ring_start(view, land, axis)
    for colour in range(3):
        view, land, axis = views(colour, 0)
        terms(colour, ring(place[axis], 1))
        terms(colour, ring(place[axis], 3))
        second[colour] = ring_second(view, land, axis)
    for colour in range(3):
        view, land, axis = views(colour, 0)
        terms(colour, place[axis])

    def piece(ref, at, rows):
        return ref.at[pl.ds(at if isinstance(at, int) else pl.multiple_of(at, 16), rows)]

    def quarters(colour, stage):
        rows = (4, 1)[stage] * ROWS[colour]
        me = place[ORDER[colour][stage + 1]]
        return [(ring(me, step) * rows, rows) for step in (2, 1, 3, 0)]

    block = core * 8 + zl * 4 + y
    last = [[], [], []]
    for stage in range(2):
        for colour in range(3):
            view, land, axis = views(colour, stage)
            me, (plus, minus) = place[axis], around[axis]
            third[colour] = []
            for way in range(2):
                first[colour][way].wait_recv()
            for at_row, rows in quarters(colour, stage):
                for way, to in ((0, plus), (1, minus)):
                    out = piece(view(way, ring(me, 3 if way else 1)), at_row, rows)
                    add(out, piece(land(way, 0), at_row, rows))
                    third[colour].append(send(out, piece(land(way, 2), at_row, rows), to))
        for step in range(4):
            for colour in range(3):
                view, land, axis = views(colour, stage)
                me = place[axis]
                if step == 0:
                    for copy in second[colour]:
                        copy.wait_recv()
                at_row, rows = quarters(colour, stage)[step]
                for way in range(2):
                    third[colour][2 * step + way].wait_recv()
                for half in range(2):
                    add(
                        piece(view(half, me), at_row, rows),
                        piece(land(1 - half, 1), at_row, rows),
                        piece(land(half, 2), at_row, rows),
                    )
                view, land, axis = views(colour, stage + 1)
                me, (plus, minus) = place[axis], around[axis]
                if stage == 1:
                    if step < 3:
                        to = across[axis] if step == 0 else (plus, minus)[step - 1]
                        for half in range(2):
                            last[colour].append(send(view(half, ring(me, (2, 1, 3)[step])), land(half, step), to))
                elif step == 0:
                    first[colour] = ring_start(view, land, axis)
                elif step == 1:
                    first[colour].append(send(view(1, ring(me, 1)), land(0, 1), plus))
                elif step == 2:
                    first[colour].append(send(view(0, ring(me, 3)), land(1, 1), minus))
        if stage == 0:
            for colour in range(3):
                first[colour], second[colour] = first[colour][:2], first[colour][2:]
    for colour in range(3):
        view, land, axis = views(colour, 2)
        for copy in last[colour]:
            copy.wait_recv()
        start, rows = START[colour], ROWS[colour]
        for half in range(2):
            total = view(half, place[axis])[...]
            for step in range(3):
                total = total + land(half, step)[...]
            yg[block, half, start : start + rows] = total

    yp, ym = around[1]

    def at(zl_of, y_of, half, start=0, rows=128):
        return yg.at[core * 8 + zl_of * 4 + y_of, half, start : start + rows]

    def pass_on(ref, to):
        return send(ref, ref, to)

    back, ahead, opposite = ring(y, 3), ring(y, 1), ring(y, 2)
    y1 = [pass_on(at(zl, y, 1), yp), pass_on(at(zl, y, 1), ym)]
    z0 = pass_on(at(zl, y, 0), zpair)
    y0 = [pass_on(at(zl, y, 0), yp), pass_on(at(zl, y, 0), ym)]
    z1 = [pass_on(at(zl, y, 1), zpair)]
    near, far = [pass_on(at(zl, y, half), partner) for half in range(2)], []
    y1[0].wait_recv()
    y1f = [pass_on(at(zl, back, 1, 0, 64), yp)]
    z1.append(pass_on(at(zl, back, 1), zpair))
    y1[1].wait_recv()
    y1f.append(pass_on(at(zl, ahead, 1, 64, 64), ym))
    z1.append(pass_on(at(zl, ahead, 1), zpair))
    z0.wait_recv()
    y0z = [pass_on(at(away, y, 0), yp), pass_on(at(away, y, 0), ym)]
    y0[0].wait_recv()
    y0f = [pass_on(at(zl, back, 0, 0, 64), yp)]
    y0[1].wait_recv()
    y0f.append(pass_on(at(zl, ahead, 0, 64, 64), ym))
    for half in (1, 0):
        near.append(pass_on(at(zl, back, half), partner))
        near.append(pass_on(at(zl, ahead, half), partner))
    far.append(pass_on(at(away, y, 0), partner))
    for copy in y1f:
        copy.wait_recv()
    z1.append(pass_on(at(zl, opposite, 1), zpair))
    near.append(pass_on(at(zl, opposite, 1), partner))
    y0z[0].wait_recv()
    y0zf = [pass_on(at(away, back, 0, 0, 64), yp)]
    y0z[1].wait_recv()
    y0zf.append(pass_on(at(away, ahead, 0, 64, 64), ym))
    for copy in y0f:
        copy.wait_recv()
    near.append(pass_on(at(zl, opposite, 0), partner))
    far.append(pass_on(at(away, back, 0), partner))
    far.append(pass_on(at(away, ahead, 0), partner))

    def subtract_coupled(zl_of):
        def round_block(i, carry):
            t = lax.div(i, 4) * 8 + zl_of * 4 + lax.rem(i, 4)
            row = pl.multiple_of(i * 128, 128)
            yh[pl.ds(row, 128), :] = jnp.concatenate([yg[t, 0], yg[t, 1]], axis=1).astype(BF16)
            return carry

        lax.fori_loop(0, 8, round_block, 0)
        lane = pl.multiple_of(zl_of * 512, 512)

        def body(tile, carry):
            row = pl.multiple_of(lax.rem(tile, 3) * 256, 256)
            b = lax.div(tile, 3)
            left = jnp.concatenate(
                [coup_v[b, pl.ds(row, 256), pl.ds(lane, 512)], coup_v[b, pl.ds(row, 256), pl.ds(lane + 1024, 512)]],
                axis=1,
            )
            seeds_v[b, pl.ds(row, 256), :] -= jnp.dot(left, yh[...], preferred_element_type=F32)
            return carry

        lax.fori_loop(0, 6, body, 0)

    for copy, y_of in zip(z1, (y, back, ahead, opposite)):
        copy.wait_recv()
        far.append(pass_on(at(away, y_of, 1), partner))
    for copy in near:
        copy.wait_recv()
    subtract_coupled(zl)
    for copy in y0zf:
        copy.wait_recv()
    far.append(pass_on(at(away, opposite, 0), partner))
    for copy in far:
        copy.wait_recv()
    store_shared = [
        load(yg.at[:, half], shared_h.at[:, :, half * 128 : half * 128 + 128]) for half in range(2)
    ]
    subtract_coupled(away)

    stores = []
    for b in range(2):
        second_hi, second_lo = split(seeds_v[b])
        for tile in range(3):
            at_row = 256 * tile
            high = inv_hi[b, at_row : at_row + 256, at_row:]
            left = jnp.concatenate([high, inv_lo[b, at_row : at_row + 256, at_row:], high], axis=1)
            right = jnp.concatenate([second_hi[at_row:], second_hi[at_row:], second_lo[at_row:]], axis=0)
            inv_v[b, at_row : at_row + 256, 0:256] = jnp.dot(left, right, preferred_element_type=F32)
        stores.append(load(inv_v.at[b, :, 0:256], priv_h.at[b]))
    for copy in (*stores, *store_shared):
        copy.wait()
    for copy in sent:
        copy.wait_send()


def on_device(private_seeds, private_inverse, coupling, shared_seed, shared_inverse):
    vmem = pltpu.VMEM
    priv, shared = pl.pallas_call(
        kernel,
        out_shape=(
            jax.ShapeDtypeStruct((2, 768, 256), F32),
            jax.ShapeDtypeStruct((16, 128, 256), F32),
        ),
        in_specs=[pl.BlockSpec(memory_space=pl.ANY)] * 5,
        out_specs=[pl.BlockSpec(memory_space=pl.ANY)] * 2,
        scratch_shapes=[
            vmem((2, 768, 256), F32),
            vmem((2, 768, 768), F32),
            vmem((2, 768, 2048), BF16),
            vmem((128, 256), F32),
            vmem((16384, 128), F32),
            *[vmem((64 * rows, 256), BF16) for rows in ROWS],
            *[vmem((64 * rows, 256), BF16) for rows in ROWS],
            vmem((2, 768, 768), BF16),
            vmem((2, 768, 768), BF16),
            vmem((256, 1536), BF16),
            vmem((2, 2, 2, 4, SY, 128), F32),
            vmem((2, 2, 2, 4, SZ, 128), F32),
            vmem((2, 2, 4, SY, 128), F32),
            vmem((2, 2, 4, SZ, 128), F32),
            vmem((2, 3, 2, SY, 128), F32),
            vmem((2, 3, SZ, 128), F32),
            vmem((2, SY, 128), F32),
            vmem((2, 4, SZ, 128), F32),
            vmem((2, 128, 256), F32),
            vmem((768, 256), BF16),
            *[vmem((126 * rows, 128), F32) for rows in ROWS],
            vmem((16, 2, 128, 128), F32),
            vmem((1024, 256), BF16),
            pltpu.SemaphoreType.DMA((16,)),
            pltpu.SemaphoreType.DMA((MESSAGES,)),
            pltpu.SemaphoreType.DMA((MESSAGES,)),
        ],
        compiler_params=pltpu.CompilerParams(
            collective_id=0, has_side_effects=True, vmem_limit_bytes=67_043_328
        ),
        name="adjoint",
    )(
        private_seeds[0, 0],
        private_inverse[0, 0],
        coupling[0],
        shared_seed[0],
        shared_inverse.reshape(16384, 128),
    )
    return priv[None, None], shared.reshape(1, 2048, 256)


def solution(mesh):
    return jax.shard_map(
        on_device,
        mesh=mesh,
        in_specs=(
            P("scen", "col", None, None, None),
            P("scen", "col", None, None, None),
            P("scen", None, None, "col"),
            P("col", "scen", None),
            P(None, None, None, "col", "scen"),
        ),
        out_specs=(P("scen", "col", None, None, None), P("col", None, None)),
        check_vma=False,
    )
```

```python
import jax
import jax.numpy as jnp
from jax import lax
from jax.experimental import pallas as pl
from jax.experimental.pallas import tpu as pltpu
from jax.sharding import PartitionSpec as P

MESH = pl.DeviceIdType.MESH
F32, BF16 = jnp.float32, jnp.bfloat16
ROWS = (32, 32, 32, 32)
START = (0, 32, 64, 96)
ORDER = ((0, 2, 1), (1, 2, 0), (2, 1, 0), (0, 1, 2))
SY, SZ = 80, 48
MESSAGES = 224


def split(value):
    high = value.astype(BF16)
    return high, (value - high.astype(F32)).astype(BF16)


def kernel(
    seeds_h, inv_h, coup_h, sseed_h, sinv_h,
    priv_h, shared_h,
    seeds_v, inv_v, coup_v, sseed_v, part, mland, mx, mh0, mh1, mh2, ml0, ml1, ml2, mxh, mxl,
    inv_hi, inv_lo, half_t, sy, sz, cy, cz, ly, lz, py, pz, rbuf, rcat, rx, rxcat, lr0, lr1, lr2, lr3, yg, yh,
    local_sem, send_sem, recv_sem,
):
    mhi, mlo, lands = (mh0, mh1, mh2), (ml0, ml1, ml2), (lr0, lr1, lr2, lr3)
    scen, col = lax.axis_index("scen"), lax.axis_index("col")
    core = lax.rem(scen, 2)
    y = lax.rem(lax.div(scen, 2), 4)
    zl = lax.div(scen, 8)
    x, zh = lax.rem(col, 4), lax.div(col, 4)
    z = zh * 2 + zl

    def device(x, y, z, core):
        return (lax.rem(z, 2) * 8 + y * 2 + core, lax.div(z, 2) * 4 + x)

    def ring(at, step):
        return lax.rem(at + step, 4)

    partner = device(x, y, z, 1 - core)
    zpair = ((1 - zl) * 8 + y * 2 + core, col)
    around = (
        (device(ring(x, 1), y, z, core), device(ring(x, 3), y, z, core)),
        (device(x, ring(y, 1), z, core), device(x, ring(y, 3), z, core)),
        (device(x, y, ring(z, 1), core), device(x, y, ring(z, 3), core)),
    )
    across = (device(ring(x, 2), y, z, core), device(x, ring(y, 2), z, core), device(x, y, ring(z, 2), core))
    crossed = [device(ring(x, step), y, z, 1 - core) for step in (2, 1, 3)]
    place = (x, y, z)

    loads = []

    def load(src, dst):
        copy = pltpu.make_async_copy(src, dst, local_sem.at[len(loads)])
        copy.start()
        loads.append(copy)
        return copy

    load_seeds = load(seeds_h, seeds_v)
    load_inv = [load(inv_h.at[b], inv_v.at[b]) for b in range(2)]
    load_coup = [load(coup_h.at[b], coup_v.at[b]) for b in range(2)]
    load_sseed = load(sseed_h, sseed_v)
    own_t, other_t = core * 8, (1 - core) * 8
    load_mx = load(sinv_h.at[pl.ds(own_t, 8), :, x, 96:128], mx.at[x, core])
    load_sinv = load(sinv_h.at[pl.ds(own_t, 8), :, :, 0:96], mland.at[core])

    barrier = pltpu.get_barrier_semaphore()
    for to in (partner, *around[0], *around[1], *around[2], *across, *crossed):
        pl.semaphore_signal(barrier, inc=1, device_id=to, device_id_type=MESH)
    pl.semaphore_wait(barrier, 13)

    sent = []

    def send(src, dst, to):
        copy = pltpu.make_async_remote_copy(
            src_ref=src,
            dst_ref=dst,
            send_sem=send_sem.at[len(sent)],
            recv_sem=recv_sem.at[len(sent)],
            device_id=to,
            device_id_type=MESH,
        )
        copy.start()
        sent.append(copy)
        return copy

    exchanged = []
    for step in (2, 1, 3):
        x_to = ring(x, step)
        for row, to_core in ((own_t, core), (other_t, 1 - core)):
            src = sinv_h.at[pl.ds(row, 8), :, x_to, 96:128]
            exchanged.append(send(src, mx.at[x, core], device(x_to, y, z, to_core)))
    exchanged.append(send(sinv_h.at[pl.ds(other_t, 8), :, x, 96:128], mx.at[x, core], partner))

    def swap_shared(half):
        return send(
            sinv_h.at[pl.ds(other_t + half * 4, 4), :, :, 0:96], mland.at[core, half * 4 : half * 4 + 4], partner
        )

    load_seeds.wait()
    for b in range(2):
        load_inv[b].wait()
        turned_hi, turned_lo = split(seeds_v[b].T)
        hi, lo = split(inv_v[b])
        inv_hi[b] = hi
        inv_lo[b] = lo
        for tile in range(3):
            depth, at = 256 * (tile + 1), 256 * tile
            left = jnp.concatenate(
                [turned_hi[:, :depth], turned_hi[:, :depth], turned_lo[:, :depth]], axis=1
            )
            right = jnp.concatenate(
                [
                    inv_hi[b, :depth, at : at + 256],
                    inv_lo[b, :depth, at : at + 256],
                    inv_hi[b, :depth, at : at + 256],
                ],
                axis=0,
            )
            first = jnp.dot(left, right, preferred_element_type=F32)
            half_t[:, b * 768 + at : b * 768 + at + 256] = first.astype(BF16)
            seeds_v[b, at : at + 256, :] = first.T

    for copy in load_coup:
        copy.wait()

    def seed_terms(zl_to):
        def body(y_to, carry):
            lane = pl.multiple_of((zl_to * 4 + y_to) * 256, 256)
            right = jnp.concatenate([coup_v[0, :, pl.ds(lane, 256)], coup_v[1, :, pl.ds(lane, 256)]], axis=0)
            out = jnp.dot(half_t[...], right, preferred_element_type=F32)
            for h in range(2):
                block = out[:, h * 128 : h * 128 + 128]
                for half in range(2):
                    sy[h, zl_to, half, y_to] = block[half * SY : half * SY + SY]
                    sz[h, zl_to, half, y_to] = block[2 * SY + half * SZ : 2 * SY + half * SZ + SZ]
            return carry

        lax.fori_loop(0, 4, body, 0)

    def add(to, *froms):
        total = to[...]
        for ref in froms:
            total = total + ref[...]
        to[...] = total

    def ring_start(view, land, axis):
        me, (plus, minus) = place[axis], around[axis]
        p1 = send(view(0, ring(me, 2)), land(0, 0), plus)
        m1 = send(view(1, ring(me, 2)), land(1, 0), minus)
        return [p1, m1]

    def ring_second(view, land, axis):
        me, (plus, minus) = place[axis], around[axis]
        p2 = send(view(1, ring(me, 1)), land(0, 1), plus)
        m2 = send(view(0, ring(me, 3)), land(1, 1), minus)
        return [p2, m2]

    def ring_third(view, land, axis, first):
        me, (plus, minus) = place[axis], around[axis]
        first[0].wait_recv()
        add(view(0, ring(me, 1)), land(0, 0))
        p3 = send(view(0, ring(me, 1)), land(0, 2), plus)
        first[1].wait_recv()
        add(view(1, ring(me, 3)), land(1, 0))
        m3 = send(view(1, ring(me, 3)), land(1, 2), minus)
        return [p3, m3]

    def ring_own(second, third):
        for copy in (*second, *third):
            copy.wait_recv()

    away = 1 - zl
    core_y, core_z = [], []
    for zl_to in (away, zl):
        seed_terms(zl_to)
        core_z.append(send(sz.at[1 - core, zl_to], cz.at[zl_to], partner))
        core_y.append(send(sy.at[1 - core, zl_to], cy.at[zl_to], partner))
    swaps = [swap_shared(half) for half in range(2)]

    def view_y(half, d):
        return sy.at[core, :, half, d]

    def view_z(half, d):
        return sz.at[core, zl, half, d]

    def land_y(way, message):
        return ly.at[way, message]

    def land_z(way, message):
        return lz.at[way, message]

    def split_shared(first, count):
        def body(block, carry):
            t, shard = lax.div(block, 8), lax.rem(block, 8)
            y_to, z_to, x_to = lax.rem(t, 4), lax.div(shard, 4) * 2 + lax.div(t, 4), lax.rem(shard, 4)
            near = mland[0, t, lax.div(shard, 4), x_to]
            far = mland[1, t, lax.div(shard, 4), x_to]
            hi, lo = split(jnp.concatenate([near, far], axis=1))
            to = (x_to, y_to, z_to)
            for colour in range(3):
                rows, start = ROWS[colour], START[colour]
                i, j, k = ORDER[colour]
                spot = pl.multiple_of(((to[i] * 4 + to[j]) * 4 + to[k]) * rows, rows)
                mhi[colour][pl.ds(spot, rows), :] = hi[start : start + rows]
                mlo[colour][pl.ds(spot, rows), :] = lo[start : start + rows]
            return carry

        lax.fori_loop(first, first + count, body, 0)

    core_z[0].wait_recv()
    add(sz.at[core, away], cz.at[away])
    pair_z = send(sz.at[core, away], pz, zpair)
    core_y[0].wait_recv()
    add(sy.at[core, away], cy.at[away])
    core_z[1].wait_recv()
    core_y[1].wait_recv()
    add(sy.at[core, zl], cy.at[zl])
    y_first = ring_start(view_y, land_y, 1)
    y_second = ring_second(view_y, land_y, 1)
    add(sz.at[core, zl], cz.at[zl])
    y_third = ring_third(view_y, land_y, 1, y_first)
    pair_z.wait_recv()
    add(sz.at[core, zl], pz)
    z_first = ring_start(view_z, land_z, 1)
    z_second = ring_second(view_z, land_z, 1)
    load_sinv.wait()
    swaps[0].wait_recv()
    split_shared(0, 32)
    ring_own(y_second, y_third)
    add(view_y(0, y), land_y(1, 1), land_y(0, 2))
    add(view_y(1, y), land_y(0, 1), land_y(1, 2))
    pair_y = [send(sy.at[core, away, half, y], py.at[half], zpair) for half in range(2)]
    z_third = ring_third(view_z, land_z, 1, z_first)
    swaps[1].wait_recv()
    split_shared(32, 32)
    pieces = []
    for half in range(2):
        pair_y[half].wait_recv()
        pieces.append(sy[core, zl, half, y] + py[half])
    ring_own(z_second, z_third)
    pieces.append(view_z(0, y)[...] + land_z(1, 1)[...] + land_z(0, 2)[...])
    pieces.append(view_z(1, y)[...] + land_z(0, 1)[...] + land_z(1, 2)[...])
    load_sseed.wait()
    rbuf[core] = sseed_v[...] - jnp.concatenate(pieces, axis=0).T
    swap_r = send(rbuf.at[core], rbuf.at[core], partner)
    gather_r = [
        send(rbuf.at[core], rx.at[x, core], to) for to in (across[0], *around[0])
    ]
    swap_r.wait_recv()
    r_hi, r_lo = split(jnp.concatenate([rbuf[0], rbuf[1]], axis=0))
    rcat[0:256] = r_hi
    rcat[256:512] = r_hi
    rcat[512:768] = r_lo

    def terms(colour, d):
        rows = ROWS[colour]
        base = 128 * START[colour]

        def body(j, carry):
            row = pl.multiple_of((d * 4 + j) * 4 * rows, 4 * rows)
            high = mhi[colour][pl.ds(row, 4 * rows), :]
            left = jnp.concatenate([high, mlo[colour][pl.ds(row, 4 * rows), :], high], axis=1)
            out = jnp.dot(left, rcat[...], preferred_element_type=F32)
            part[pl.ds(pl.multiple_of(base + row, rows), 4 * rows), :] = out[:, :128]
            part[pl.ds(pl.multiple_of(base + 64 * rows + row, rows), 4 * rows), :] = out[:, 128:]
            return carry

        lax.fori_loop(0, 4, body, 0)

    def views(colour, stage):
        rows = ROWS[colour]
        axes = ORDER[colour]
        size = (16, 4, 1)[stage] * rows
        half_size = (16 if colour == 3 else 64) * rows
        base = 128 * START[colour]
        for step in range(colour == 3, stage):
            base = base + place[axes[step]] * ((16, 4)[step] * rows)

        def view(half, d):
            return part.at[pl.ds(pl.multiple_of(base + half * half_size + d * size, 16), size)]

        span = (5 if colour == 3 else 21) * rows
        shift = ((0, 0, 4) if colour == 3 else (0, 16, 20))[stage] * rows

        def land(way, message):
            return lands[colour].at[pl.ds((way * 3 + message) * span + shift, size)]

        return view, land, axes[stage]

    def piece(ref, at_row, rows):
        return ref.at[pl.ds(pl.multiple_of(at_row, 16), rows)]

    def quarters(colour, stage):
        rows = (4, 1)[stage] * ROWS[colour]
        me = place[ORDER[colour][stage + 1]]
        return [(ring(me, step) * rows, rows) for step in (2, 1, 3, 0)]

    first, second, third, last = {}, {}, {}, {}

    def pass_sums(colour, stage):
        view, land, axis = views(colour, stage)
        me, (plus, minus) = place[axis], around[axis]
        third[colour] = []
        for way in range(2):
            first[colour][way].wait_recv()
        for at_row, rows in quarters(colour, stage):
            for way, to in ((0, plus), (1, minus)):
                out = piece(view(way, ring(me, 3 if way else 1)), at_row, rows)
                add(out, piece(land(way, 0), at_row, rows))
                third[colour].append(send(out, piece(land(way, 2), at_row, rows), to))

    def own_sums(colour, stage, step):
        view, land, axis = views(colour, stage)
        me = place[axis]
        if step == 0:
            for copy in second[colour]:
                copy.wait_recv()
            ready[colour] = []
            last[colour] = []
        at_row, rows = quarters(colour, stage)[step]
        for way in range(2):
            third[colour][2 * step + way].wait_recv()
        for half in range(2):
            add(
                piece(view(half, me), at_row, rows),
                piece(land(1 - half, 1), at_row, rows),
                piece(land(half, 2), at_row, rows),
            )
        view, land, axis = views(colour, stage + 1)
        me, (plus, minus) = place[axis], around[axis]
        if stage == 1:
            if step < 3:
                to = (across[axis], plus, minus)[step]
                for half in range(2):
                    last[colour].append(send(view(half, ring(me, (2, 1, 3)[step])), land(half, step), to))
        elif step == 0:
            ready[colour] = ring_start(view, land, axis)
        elif step == 1:
            ready[colour].append(send(view(1, ring(me, 1)), land(0, 1), plus))
        elif step == 2:
            ready[colour].append(send(view(0, ring(me, 3)), land(1, 1), minus))
        else:
            first[colour], second[colour] = ready[colour][:2], ready[colour][2:]

    ready = {}
    for colour in (1, 2, 0):
        view, land, axis = views(colour, 0)
        terms(colour, ring(place[axis], 2))
        first[colour] = ring_start(view, land, axis)
    for colour in (1, 2, 0):
        view, land, axis = views(colour, 0)
        terms(colour, ring(place[axis], 1))
        terms(colour, ring(place[axis], 3))
        second[colour] = ring_second(view, land, axis)
    for colour in (1, 2, 0):
        terms(colour, place[ORDER[colour][0]])
    load_mx.wait()
    for copy in exchanged:
        copy.wait_recv()

    def split_exchanged(block, carry):
        t, zh_of = lax.div(block, 2), lax.rem(block, 2)
        hi, lo = split(jnp.concatenate([mx[i, j, t, zh_of] for i in range(4) for j in range(2)], axis=1))
        row = pl.multiple_of((lax.rem(t, 4) * 4 + zh_of * 2 + lax.div(t, 4)) * 32, 32)
        mxh[pl.ds(row, 32), :] = hi
        mxl[pl.ds(row, 32), :] = lo
        return carry

    lax.fori_loop(0, 16, split_exchanged, 0)
    pass_sums(1, 0)
    pass_sums(2, 0)
    relayed = []
    for copy, step in zip(gather_r, (2, 3, 1)):
        copy.wait_recv()
        spot = rx.at[ring(x, step), core]
        relayed.append(send(spot, spot, partner))
    rx[x] = rbuf[...]
    for copy in relayed:
        copy.wait_recv()
    for i in range(8):
        hi, lo = split(rx[i // 2, i % 2])
        rxcat[i * 128 : i * 128 + 128] = hi
        rxcat[1024 + i * 128 : 1152 + i * 128] = lo

    def exchanged_terms(j, carry):
        row = pl.multiple_of(j * 128, 128)
        high, low = mxh[pl.ds(row, 128), :], mxl[pl.ds(row, 128), :]
        out = jnp.dot(high, rxcat[0:1024], preferred_element_type=F32)
        out += jnp.dot(low, rxcat[0:1024], preferred_element_type=F32)
        out += jnp.dot(high, rxcat[1024:2048], preferred_element_type=F32)
        part[pl.ds(pl.multiple_of(12288 + row, 128), 128), :] = out[:, :128]
        part[pl.ds(pl.multiple_of(12800 + row, 128), 128), :] = out[:, 128:]
        return carry

    lax.fori_loop(0, 4, exchanged_terms, 0)
    view, land, axis = views(3, 1)
    first[3] = ring_start(view, land, axis)
    second[3] = ring_second(view, land, axis)
    pass_sums(0, 0)
    for step in range(4):
        own_sums(1, 0, step)
        own_sums(2, 0, step)
    pass_sums(3, 1)
    pass_sums(1, 1)
    pass_sums(2, 1)
    for step in range(4):
        own_sums(0, 0, step)
    for step in range(4):
        for colour in (3, 1, 2):
            own_sums(colour, 1, step)
    pass_sums(0, 1)
    for step in range(4):
        own_sums(0, 1, step)
    block = core * 8 + zl * 4 + y
    for colour in (3, 1, 2, 0):
        view, land, axis = views(colour, 2)
        for copy in last[colour]:
            copy.wait_recv()
        start, rows = START[colour], ROWS[colour]
        for half in range(2):
            total = view(half, place[axis])[...]
            for step in range(3):
                total = total + land(half, step)[...]
            yg[block, half, start : start + rows] = total

    yp, ym = around[1]

    def at(zl_of, y_of, half, start=0, rows=128):
        return yg.at[core * 8 + zl_of * 4 + y_of, half, start : start + rows]

    def pass_on(ref, to):
        return send(ref, ref, to)

    back, ahead, opposite = ring(y, 3), ring(y, 1), ring(y, 2)
    y1 = [pass_on(at(zl, y, 1), yp), pass_on(at(zl, y, 1), ym)]
    z0 = pass_on(at(zl, y, 0), zpair)
    y0 = [pass_on(at(zl, y, 0), yp), pass_on(at(zl, y, 0), ym)]
    z1 = [pass_on(at(zl, y, 1), zpair)]
    near, far = [pass_on(at(zl, y, half), partner) for half in range(2)], []
    y1[0].wait_recv()
    y1f = [pass_on(at(zl, back, 1, 0, 64), yp)]
    z1.append(pass_on(at(zl, back, 1), zpair))
    y1[1].wait_recv()
    y1f.append(pass_on(at(zl, ahead, 1, 64, 64), ym))
    z1.append(pass_on(at(zl, ahead, 1), zpair))
    z0.wait_recv()
    y0z = [pass_on(at(away, y, 0), yp), pass_on(at(away, y, 0), ym)]
    y0[0].wait_recv()
    y0f = [pass_on(at(zl, back, 0, 0, 64), yp)]
    y0[1].wait_recv()
    y0f.append(pass_on(at(zl, ahead, 0, 64, 64), ym))
    for half in (1, 0):
        near.append(pass_on(at(zl, back, half), partner))
        near.append(pass_on(at(zl, ahead, half), partner))
    far.append(pass_on(at(away, y, 0), partner))
    for copy in y1f:
        copy.wait_recv()
    z1.append(pass_on(at(zl, opposite, 1), zpair))
    near.append(pass_on(at(zl, opposite, 1), partner))
    y0z[0].wait_recv()
    y0zf = [pass_on(at(away, back, 0, 0, 64), yp)]
    y0z[1].wait_recv()
    y0zf.append(pass_on(at(away, ahead, 0, 64, 64), ym))
    for copy in y0f:
        copy.wait_recv()
    near.append(pass_on(at(zl, opposite, 0), partner))
    far.append(pass_on(at(away, back, 0), partner))
    far.append(pass_on(at(away, ahead, 0), partner))

    def subtract_coupled(zl_of):
        def round_block(i, carry):
            t = lax.div(i, 4) * 8 + zl_of * 4 + lax.rem(i, 4)
            row = pl.multiple_of(i * 128, 128)
            yh[pl.ds(row, 128), :] = jnp.concatenate([yg[t, 0], yg[t, 1]], axis=1).astype(BF16)
            return carry

        lax.fori_loop(0, 8, round_block, 0)
        lane = pl.multiple_of(zl_of * 512, 512)

        def body(tile, carry):
            row = pl.multiple_of(lax.rem(tile, 3) * 256, 256)
            b = lax.div(tile, 3)
            left = jnp.concatenate(
                [coup_v[b, pl.ds(row, 256), pl.ds(lane, 512)], coup_v[b, pl.ds(row, 256), pl.ds(lane + 1024, 512)]],
                axis=1,
            )
            seeds_v[b, pl.ds(row, 256), :] -= jnp.dot(left, yh[...], preferred_element_type=F32)
            return carry

        lax.fori_loop(0, 6, body, 0)

    for copy, y_of in zip(z1, (y, back, ahead, opposite)):
        copy.wait_recv()
        far.append(pass_on(at(away, y_of, 1), partner))
    for copy in near:
        copy.wait_recv()
    subtract_coupled(zl)
    for copy in y0zf:
        copy.wait_recv()
    far.append(pass_on(at(away, opposite, 0), partner))
    for copy in far:
        copy.wait_recv()
    store_shared = [
        load(yg.at[:, half], shared_h.at[:, :, half * 128 : half * 128 + 128]) for half in range(2)
    ]
    subtract_coupled(away)

    stores = []
    for b in range(2):
        second_hi, second_lo = split(seeds_v[b])
        for tile in range(3):
            at_row = 256 * tile
            high = inv_hi[b, at_row : at_row + 256, at_row:]
            left = jnp.concatenate([high, inv_lo[b, at_row : at_row + 256, at_row:], high], axis=1)
            right = jnp.concatenate([second_hi[at_row:], second_hi[at_row:], second_lo[at_row:]], axis=0)
            inv_v[b, at_row : at_row + 256, 0:256] = jnp.dot(left, right, preferred_element_type=F32)
        stores.append(load(inv_v.at[b, :, 0:256], priv_h.at[b]))
    for copy in (*stores, *store_shared):
        copy.wait()
    for copy in sent:
        copy.wait_send()


def on_device(private_seeds, private_inverse, coupling, shared_seed, shared_inverse):
    vmem = pltpu.VMEM
    priv, shared = pl.pallas_call(
        kernel,
        out_shape=(
            jax.ShapeDtypeStruct((2, 768, 256), F32),
            jax.ShapeDtypeStruct((16, 128, 256), F32),
        ),
        in_specs=[pl.BlockSpec(memory_space=pl.ANY)] * 5,
        out_specs=[pl.BlockSpec(memory_space=pl.ANY)] * 2,
        scratch_shapes=[
            vmem((2, 768, 256), F32),
            vmem((2, 768, 768), F32),
            vmem((2, 768, 2048), BF16),
            vmem((128, 256), F32),
            vmem((13312, 128), F32),
            vmem((2, 8, 2, 4, 96, 128), F32),
            vmem((4, 2, 8, 2, 32, 128), F32),
            *[vmem((2048, 256), BF16)] * 6,
            *[vmem((512, 1024), BF16)] * 2,
            vmem((2, 768, 768), BF16),
            vmem((2, 768, 768), BF16),
            vmem((256, 1536), BF16),
            vmem((2, 2, 2, 4, SY, 128), F32),
            vmem((2, 2, 2, 4, SZ, 128), F32),
            vmem((2, 2, 4, SY, 128), F32),
            vmem((2, 2, 4, SZ, 128), F32),
            vmem((2, 3, 2, SY, 128), F32),
            vmem((2, 3, SZ, 128), F32),
            vmem((2, SY, 128), F32),
            vmem((2, 4, SZ, 128), F32),
            vmem((2, 128, 256), F32),
            vmem((768, 256), BF16),
            vmem((4, 2, 128, 256), F32),
            vmem((2048, 256), BF16),
            *[vmem((126 * 32, 128), F32)] * 3,
            vmem((30 * 32, 128), F32),
            vmem((16, 2, 128, 128), F32),
            vmem((1024, 256), BF16),
            pltpu.SemaphoreType.DMA((16,)),
            pltpu.SemaphoreType.DMA((MESSAGES,)),
            pltpu.SemaphoreType.DMA((MESSAGES,)),
        ],
        compiler_params=pltpu.CompilerParams(
            collective_id=0, has_side_effects=True, vmem_limit_bytes=67_043_328
        ),
        name="adjoint",
    )(
        private_seeds[0, 0],
        private_inverse[0, 0],
        coupling[0],
        shared_seed[0],
        shared_inverse.reshape(16, 2, 4, 128, 128),
    )
    return priv[None, None], shared.reshape(1, 2048, 256)


def solution(mesh):
    return jax.shard_map(
        on_device,
        mesh=mesh,
        in_specs=(
            P("scen", "col", None, None, None),
            P("scen", "col", None, None, None),
            P("scen", None, None, "col"),
            P("col", "scen", None),
            P(None, None, None, "col", "scen"),
        ),
        out_specs=(P("scen", "col", None, None, None), P("col", None, None)),
        check_vma=False,
    )
```

```python
import jax
import jax.numpy as jnp
from jax import lax
from jax.experimental import pallas as pl
from jax.experimental.pallas import tpu as pltpu
from jax.sharding import PartitionSpec as P

MESH = pl.DeviceIdType.MESH
F32, BF16 = jnp.float32, jnp.bfloat16
ROWS = (32, 32, 32, 32)
START = (0, 32, 64, 96)
ORDER = ((0, 2, 1), (1, 2, 0), (2, 1, 0), (0, 1, 2))
SY, SZ = 80, 48
MESSAGES = 256


def split(value):
    high = value.astype(BF16)
    return high, (value - high.astype(F32)).astype(BF16)


def kernel(
    seeds_h, inv_h, coup_h, sseed_h, sinv_h,
    priv_h, shared_h,
    seeds_v, inv_v, coup_v, sseed_v, part, mland, mx, mh0, mh1, mh2, ml0, ml1, ml2, mxh, mxl,
    inv_hi, inv_lo, half_t, sy, sz, cy, cz, ly, lz, py, pz, rbuf, rcat, rx, rxcat, lr0, lr1, lr2, lr3, yg, yh,
    local_sem, send_sem, recv_sem,
):
    mhi, mlo, lands = (mh0, mh1, mh2), (ml0, ml1, ml2), (lr0, lr1, lr2, lr3)
    scen, col = lax.axis_index("scen"), lax.axis_index("col")
    core = lax.rem(scen, 2)
    y = lax.rem(lax.div(scen, 2), 4)
    zl = lax.div(scen, 8)
    x, zh = lax.rem(col, 4), lax.div(col, 4)
    z = zh * 2 + zl

    def device(x, y, z, core):
        return (lax.rem(z, 2) * 8 + y * 2 + core, lax.div(z, 2) * 4 + x)

    def ring(at, step):
        return lax.rem(at + step, 4)

    partner = device(x, y, z, 1 - core)
    zpair = ((1 - zl) * 8 + y * 2 + core, col)
    around = (
        (device(ring(x, 1), y, z, core), device(ring(x, 3), y, z, core)),
        (device(x, ring(y, 1), z, core), device(x, ring(y, 3), z, core)),
        (device(x, y, ring(z, 1), core), device(x, y, ring(z, 3), core)),
    )
    across = (device(ring(x, 2), y, z, core), device(x, ring(y, 2), z, core), device(x, y, ring(z, 2), core))
    crossed = [device(ring(x, step), y, z, 1 - core) for step in (2, 1, 3)]
    place = (x, y, z)

    loads = []

    def load(src, dst):
        copy = pltpu.make_async_copy(src, dst, local_sem.at[len(loads)])
        copy.start()
        loads.append(copy)
        return copy

    load_seeds = load(seeds_h, seeds_v)
    load_inv = [load(inv_h.at[b], inv_v.at[b]) for b in range(2)]
    load_coup = [load(coup_h.at[b], coup_v.at[b]) for b in range(2)]
    load_sseed = load(sseed_h, sseed_v)
    own_t, other_t = core * 8, (1 - core) * 8
    load_mx = load(sinv_h.at[pl.ds(own_t, 8), :, x, 96:128], mx.at[x, core])
    load_sinv = load(sinv_h.at[pl.ds(own_t, 8), :, :, 0:96], mland.at[core])

    barrier = pltpu.get_barrier_semaphore()
    for to in (partner, *around[0], *around[1], *around[2], *across, *crossed):
        pl.semaphore_signal(barrier, inc=1, device_id=to, device_id_type=MESH)
    pl.semaphore_wait(barrier, 13)

    sent = []

    def send(src, dst, to):
        copy = pltpu.make_async_remote_copy(
            src_ref=src,
            dst_ref=dst,
            send_sem=send_sem.at[len(sent)],
            recv_sem=recv_sem.at[len(sent)],
            device_id=to,
            device_id_type=MESH,
        )
        copy.start()
        sent.append(copy)
        return copy

    exchanged = []
    for step in (2, 1, 3):
        x_to = ring(x, step)
        for row, to_core in ((own_t, core), (other_t, 1 - core)):
            src = sinv_h.at[pl.ds(row, 8), :, x_to, 96:128]
            exchanged.append(send(src, mx.at[x, core], device(x_to, y, z, to_core)))
    exchanged.append(send(sinv_h.at[pl.ds(other_t, 8), :, x, 96:128], mx.at[x, core], partner))

    def swap_shared(half):
        return send(
            sinv_h.at[pl.ds(other_t + half * 4, 4), :, :, 0:96], mland.at[core, half * 4 : half * 4 + 4], partner
        )

    load_seeds.wait()
    for b in range(2):
        load_inv[b].wait()
        turned_hi, turned_lo = split(seeds_v[b].T)
        hi, lo = split(inv_v[b])
        inv_hi[b] = hi
        inv_lo[b] = lo
        for tile in range(3):
            depth, at = 256 * (tile + 1), 256 * tile
            left = jnp.concatenate(
                [turned_hi[:, :depth], turned_hi[:, :depth], turned_lo[:, :depth]], axis=1
            )
            right = jnp.concatenate(
                [
                    inv_hi[b, :depth, at : at + 256],
                    inv_lo[b, :depth, at : at + 256],
                    inv_hi[b, :depth, at : at + 256],
                ],
                axis=0,
            )
            first = jnp.dot(left, right, preferred_element_type=F32)
            half_t[:, b * 768 + at : b * 768 + at + 256] = first.astype(BF16)
            seeds_v[b, at : at + 256, :] = first.T

    for copy in load_coup:
        copy.wait()

    def seed_terms(zl_to):
        def body(y_to, carry):
            lane = pl.multiple_of((zl_to * 4 + y_to) * 256, 256)
            right = jnp.concatenate([coup_v[0, :, pl.ds(lane, 256)], coup_v[1, :, pl.ds(lane, 256)]], axis=0)
            out = jnp.dot(half_t[...], right, preferred_element_type=F32)
            for h in range(2):
                block = out[:, h * 128 : h * 128 + 128]
                for half in range(2):
                    sy[h, zl_to, half, y_to] = block[half * SY : half * SY + SY]
                    sz[h, zl_to, half, y_to] = block[2 * SY + half * SZ : 2 * SY + half * SZ + SZ]
            return carry

        lax.fori_loop(0, 4, body, 0)

    def add(to, *froms):
        total = to[...]
        for ref in froms:
            total = total + ref[...]
        to[...] = total

    def ring_start(view, land, axis):
        me, (plus, minus) = place[axis], around[axis]
        p1 = send(view(0, ring(me, 2)), land(0, 0), plus)
        m1 = send(view(1, ring(me, 2)), land(1, 0), minus)
        return [p1, m1]

    def ring_second(view, land, axis):
        me, (plus, minus) = place[axis], around[axis]
        p2 = send(view(1, ring(me, 1)), land(0, 1), plus)
        m2 = send(view(0, ring(me, 3)), land(1, 1), minus)
        return [p2, m2]

    def ring_third(view, land, axis, first):
        me, (plus, minus) = place[axis], around[axis]
        first[0].wait_recv()
        add(view(0, ring(me, 1)), land(0, 0))
        p3 = send(view(0, ring(me, 1)), land(0, 2), plus)
        first[1].wait_recv()
        add(view(1, ring(me, 3)), land(1, 0))
        m3 = send(view(1, ring(me, 3)), land(1, 2), minus)
        return [p3, m3]

    def ring_own(second, third):
        for copy in (*second, *third):
            copy.wait_recv()

    away = 1 - zl
    core_y, core_z = [], []
    for zl_to in (away, zl):
        seed_terms(zl_to)
        core_z.append(send(sz.at[1 - core, zl_to], cz.at[zl_to], partner))
        core_y.append(send(sy.at[1 - core, zl_to], cy.at[zl_to], partner))
    swaps = [swap_shared(half) for half in range(2)]

    def view_y(half, d):
        return sy.at[core, :, half, d]

    def view_z(half, d):
        return sz.at[core, zl, half, d]

    def land_y(way, message):
        return ly.at[way, message]

    def land_z(way, message):
        return lz.at[way, message]

    def split_shared(first, count):
        def body(block, carry):
            t, shard = lax.div(block, 8), lax.rem(block, 8)
            y_to, z_to, x_to = lax.rem(t, 4), lax.div(shard, 4) * 2 + lax.div(t, 4), lax.rem(shard, 4)
            near = mland[0, t, lax.div(shard, 4), x_to]
            far = mland[1, t, lax.div(shard, 4), x_to]
            hi, lo = split(jnp.concatenate([near, far], axis=1))
            to = (x_to, y_to, z_to)
            for colour in range(3):
                rows, start = ROWS[colour], START[colour]
                i, j, k = ORDER[colour]
                spot = pl.multiple_of(((to[i] * 4 + to[j]) * 4 + to[k]) * rows, rows)
                mhi[colour][pl.ds(spot, rows), :] = hi[start : start + rows]
                mlo[colour][pl.ds(spot, rows), :] = lo[start : start + rows]
            return carry

        lax.fori_loop(first, first + count, body, 0)

    core_z[0].wait_recv()
    add(sz.at[core, away], cz.at[away])
    pair_z = send(sz.at[core, away], pz, zpair)
    core_y[0].wait_recv()
    add(sy.at[core, away], cy.at[away])
    core_z[1].wait_recv()
    core_y[1].wait_recv()
    add(sy.at[core, zl], cy.at[zl])
    y_first = ring_start(view_y, land_y, 1)
    y_second = ring_second(view_y, land_y, 1)
    add(sz.at[core, zl], cz.at[zl])
    y_third = ring_third(view_y, land_y, 1, y_first)
    pair_z.wait_recv()
    add(sz.at[core, zl], pz)
    z_first = ring_start(view_z, land_z, 1)
    z_second = ring_second(view_z, land_z, 1)
    load_sinv.wait()
    swaps[0].wait_recv()
    split_shared(0, 32)
    ring_own(y_second, y_third)
    add(view_y(0, y), land_y(1, 1), land_y(0, 2))
    add(view_y(1, y), land_y(0, 1), land_y(1, 2))
    pair_y = [send(sy.at[core, away, half, y], py.at[half], zpair) for half in range(2)]
    z_third = ring_third(view_z, land_z, 1, z_first)
    swaps[1].wait_recv()
    split_shared(32, 32)
    pieces = []
    for half in range(2):
        pair_y[half].wait_recv()
        pieces.append(sy[core, zl, half, y] + py[half])
    ring_own(z_second, z_third)
    pieces.append(view_z(0, y)[...] + land_z(1, 1)[...] + land_z(0, 2)[...])
    pieces.append(view_z(1, y)[...] + land_z(0, 1)[...] + land_z(1, 2)[...])
    load_sseed.wait()
    rbuf[core] = sseed_v[...] - jnp.concatenate(pieces, axis=0).T
    swap_r = send(rbuf.at[core], rbuf.at[core], partner)
    gather_r = [
        send(rbuf.at[core], rx.at[x, core], to) for to in (across[0], *around[0])
    ]
    swap_r.wait_recv()
    r_hi, r_lo = split(jnp.concatenate([rbuf[0], rbuf[1]], axis=0))
    rcat[0:256] = r_hi
    rcat[256:512] = r_hi
    rcat[512:768] = r_lo

    def terms(colour, d):
        rows = ROWS[colour]
        base = 128 * START[colour]

        def body(j, carry):
            row = pl.multiple_of((d * 4 + j) * 4 * rows, 4 * rows)
            high = mhi[colour][pl.ds(row, 4 * rows), :]
            left = jnp.concatenate([high, mlo[colour][pl.ds(row, 4 * rows), :], high], axis=1)
            out = jnp.dot(left, rcat[...], preferred_element_type=F32)
            part[pl.ds(pl.multiple_of(base + row, rows), 4 * rows), :] = out[:, :128]
            part[pl.ds(pl.multiple_of(base + 64 * rows + row, rows), 4 * rows), :] = out[:, 128:]
            return carry

        lax.fori_loop(0, 4, body, 0)

    def views(colour, stage):
        rows = ROWS[colour]
        axes = ORDER[colour]
        size = (16, 4, 1)[stage] * rows
        half_size = (16 if colour == 3 else 64) * rows
        base = 128 * START[colour]
        for step in range(colour == 3, stage):
            base = base + place[axes[step]] * ((16, 4)[step] * rows)

        def view(half, d):
            return part.at[pl.ds(pl.multiple_of(base + half * half_size + d * size, 16), size)]

        span = (5 if colour == 3 else 21) * rows
        shift = ((0, 0, 4) if colour == 3 else (0, 16, 20))[stage] * rows

        def land(way, message):
            return lands[colour].at[pl.ds((way * 3 + message) * span + shift, size)]

        return view, land, axes[stage]

    def piece(ref, at_row, rows):
        return ref.at[pl.ds(pl.multiple_of(at_row, 16), rows)]

    def quarters(colour, stage):
        rows = (4, 1)[stage] * ROWS[colour]
        me = place[ORDER[colour][stage + 1]]
        return [(ring(me, step) * rows, rows) for step in (2, 1, 3, 0)]

    first, second, third, last = {}, {}, {}, {}

    def pass_sums(colour, stage):
        view, land, axis = views(colour, stage)
        me, (plus, minus) = place[axis], around[axis]
        third[colour] = []
        for way in range(2):
            first[colour][way].wait_recv()
        for at_row, rows in quarters(colour, stage):
            for way, to in ((0, plus), (1, minus)):
                out = piece(view(way, ring(me, 3 if way else 1)), at_row, rows)
                add(out, piece(land(way, 0), at_row, rows))
                third[colour].append(send(out, piece(land(way, 2), at_row, rows), to))

    def own_sums(colour, stage, step):
        view, land, axis = views(colour, stage)
        me = place[axis]
        if step == 0:
            for copy in second[colour]:
                copy.wait_recv()
            ready[colour] = []
            last[colour] = []
        at_row, rows = quarters(colour, stage)[step]
        for way in range(2):
            third[colour][2 * step + way].wait_recv()
        for half in range(2):
            add(
                piece(view(half, me), at_row, rows),
                piece(land(1 - half, 1), at_row, rows),
                piece(land(half, 2), at_row, rows),
            )
        view, land, axis = views(colour, stage + 1)
        me, (plus, minus) = place[axis], around[axis]
        if stage == 1:
            if step < 3:
                to = (across[axis], plus, minus)[step]
                for half in range(2):
                    last[colour].append(send(view(half, ring(me, (2, 1, 3)[step])), land(half, step), to))
        elif step == 0:
            ready[colour] = ring_start(view, land, axis)
        elif step == 1:
            ready[colour].append(send(view(1, ring(me, 1)), land(0, 1), plus))
        elif step == 2:
            ready[colour].append(send(view(0, ring(me, 3)), land(1, 1), minus))
        else:
            first[colour], second[colour] = ready[colour][:2], ready[colour][2:]

    yp, ym = around[1]
    back, ahead, opposite = ring(y, 3), ring(y, 1), ring(y, 2)
    block = core * 8 + zl * 4 + y

    def pass_on(ref, to):
        return send(ref, ref, to)

    def gather(start, rows, near, far):
        def at(zl_of, y_of, half, part_of=None):
            first_row, count = start, rows
            if part_of is not None:
                first_row, count = start + part_of * (rows // 2), rows // 2
            return yg.at[core * 8 + zl_of * 4 + y_of, half, first_row : first_row + count]

        y1 = [pass_on(at(zl, y, 1), yp), pass_on(at(zl, y, 1), ym)]
        z0 = pass_on(at(zl, y, 0), zpair)
        y0 = [pass_on(at(zl, y, 0), yp), pass_on(at(zl, y, 0), ym)]
        z1 = [pass_on(at(zl, y, 1), zpair)]
        for half in range(2):
            near.append(pass_on(at(zl, y, half), partner))
        yield
        y1[0].wait_recv()
        y1f = [pass_on(at(zl, back, 1, 0), yp)]
        z1.append(pass_on(at(zl, back, 1), zpair))
        y1[1].wait_recv()
        y1f.append(pass_on(at(zl, ahead, 1, 1), ym))
        z1.append(pass_on(at(zl, ahead, 1), zpair))
        z0.wait_recv()
        y0z = [pass_on(at(away, y, 0), yp), pass_on(at(away, y, 0), ym)]
        y0[0].wait_recv()
        y0f = [pass_on(at(zl, back, 0, 0), yp)]
        y0[1].wait_recv()
        y0f.append(pass_on(at(zl, ahead, 0, 1), ym))
        for half in (1, 0):
            near.append(pass_on(at(zl, back, half), partner))
            near.append(pass_on(at(zl, ahead, half), partner))
        far.append(pass_on(at(away, y, 0), partner))
        yield
        for copy in y1f:
            copy.wait_recv()
        z1.append(pass_on(at(zl, opposite, 1), zpair))
        near.append(pass_on(at(zl, opposite, 1), partner))
        y0z[0].wait_recv()
        y0zf = [pass_on(at(away, back, 0, 0), yp)]
        y0z[1].wait_recv()
        y0zf.append(pass_on(at(away, ahead, 0, 1), ym))
        for copy in y0f:
            copy.wait_recv()
        near.append(pass_on(at(zl, opposite, 0), partner))
        far.append(pass_on(at(away, back, 0), partner))
        far.append(pass_on(at(away, ahead, 0), partner))
        yield
        for copy, y_of in zip(z1, (y, back, ahead, opposite)):
            copy.wait_recv()
            far.append(pass_on(at(away, y_of, 1), partner))
        for copy in y0zf:
            copy.wait_recv()
        far.append(pass_on(at(away, opposite, 0), partner))

    def total_sums(colour):
        view, land, axis = views(colour, 2)
        for copy in last[colour]:
            copy.wait_recv()
        start, rows = START[colour], ROWS[colour]
        for half in range(2):
            total = view(half, place[axis])[...]
            for step in range(3):
                total = total + land(half, step)[...]
            yg[block, half, start : start + rows] = total

    ready = {}
    for colour in (1, 2, 0):
        view, land, axis = views(colour, 0)
        terms(colour, ring(place[axis], 2))
        first[colour] = ring_start(view, land, axis)
    for colour in (1, 2, 0):
        view, land, axis = views(colour, 0)
        terms(colour, ring(place[axis], 1))
        terms(colour, ring(place[axis], 3))
        second[colour] = ring_second(view, land, axis)
    for colour in (1, 2, 0):
        terms(colour, place[ORDER[colour][0]])
    load_mx.wait()
    for copy in exchanged:
        copy.wait_recv()

    def split_exchanged(block, carry):
        t, zh_of = lax.div(block, 2), lax.rem(block, 2)
        hi, lo = split(jnp.concatenate([mx[i, j, t, zh_of] for i in range(4) for j in range(2)], axis=1))
        row = pl.multiple_of((lax.rem(t, 4) * 4 + zh_of * 2 + lax.div(t, 4)) * 32, 32)
        mxh[pl.ds(row, 32), :] = hi
        mxl[pl.ds(row, 32), :] = lo
        return carry

    lax.fori_loop(0, 16, split_exchanged, 0)
    pass_sums(1, 0)
    pass_sums(2, 0)
    relayed = []
    for copy, step in zip(gather_r, (2, 3, 1)):
        copy.wait_recv()
        spot = rx.at[ring(x, step), core]
        relayed.append(send(spot, spot, partner))
    rx[x] = rbuf[...]
    for copy in relayed:
        copy.wait_recv()
    for i in range(8):
        hi, lo = split(rx[i // 2, i % 2])
        rxcat[i * 128 : i * 128 + 128] = hi
        rxcat[1024 + i * 128 : 1152 + i * 128] = lo

    def exchanged_terms(j, carry):
        row = pl.multiple_of(j * 128, 128)
        high, low = mxh[pl.ds(row, 128), :], mxl[pl.ds(row, 128), :]
        out = jnp.dot(high, rxcat[0:1024], preferred_element_type=F32)
        out += jnp.dot(low, rxcat[0:1024], preferred_element_type=F32)
        out += jnp.dot(high, rxcat[1024:2048], preferred_element_type=F32)
        part[pl.ds(pl.multiple_of(12288 + row, 128), 128), :] = out[:, :128]
        part[pl.ds(pl.multiple_of(12800 + row, 128), 128), :] = out[:, 128:]
        return carry

    lax.fori_loop(0, 4, exchanged_terms, 0)
    view, land, axis = views(3, 1)
    first[3] = ring_start(view, land, axis)
    second[3] = ring_second(view, land, axis)
    pass_sums(0, 0)
    for step in range(4):
        own_sums(1, 0, step)
        own_sums(2, 0, step)
    pass_sums(1, 1)
    pass_sums(2, 1)
    pass_sums(3, 1)
    for step in range(4):
        own_sums(0, 0, step)
    for step in range(4):
        for colour in (1, 2):
            own_sums(colour, 1, step)
    near, far = [], []
    early = gather(32, 96, near, far)
    late = gather(0, 32, near, far)
    pass_sums(0, 1)
    for step in range(4):
        own_sums(3, 1, step)
    for step in range(4):
        own_sums(0, 1, step)
    for colour in (1, 2, 3):
        total_sums(colour)
    next(early)
    total_sums(0)
    next(late)
    next(early)
    next(late)
    next(early)
    next(late)
    for _ in early:
        pass

    def subtract_coupled(zl_of):
        def round_block(i, carry):
            t = lax.div(i, 4) * 8 + zl_of * 4 + lax.rem(i, 4)
            row = pl.multiple_of(i * 128, 128)
            yh[pl.ds(row, 128), :] = jnp.concatenate([yg[t, 0], yg[t, 1]], axis=1).astype(BF16)
            return carry

        lax.fori_loop(0, 8, round_block, 0)
        lane = pl.multiple_of(zl_of * 512, 512)

        def body(tile, carry):
            row = pl.multiple_of(lax.rem(tile, 3) * 256, 256)
            b = lax.div(tile, 3)
            left = jnp.concatenate(
                [coup_v[b, pl.ds(row, 256), pl.ds(lane, 512)], coup_v[b, pl.ds(row, 256), pl.ds(lane + 1024, 512)]],
                axis=1,
            )
            seeds_v[b, pl.ds(row, 256), :] -= jnp.dot(left, yh[...], preferred_element_type=F32)
            return carry

        lax.fori_loop(0, 6, body, 0)

    for copy in near:
        copy.wait_recv()
    subtract_coupled(zl)
    for _ in late:
        pass
    for copy in far:
        copy.wait_recv()
    store_shared = [
        load(yg.at[:, half], shared_h.at[:, :, half * 128 : half * 128 + 128]) for half in range(2)
    ]
    subtract_coupled(away)

    stores = []
    for b in range(2):
        second_hi, second_lo = split(seeds_v[b])
        for tile in range(3):
            at_row = 256 * tile
            high = inv_hi[b, at_row : at_row + 256, at_row:]
            left = jnp.concatenate([high, inv_lo[b, at_row : at_row + 256, at_row:], high], axis=1)
            right = jnp.concatenate([second_hi[at_row:], second_hi[at_row:], second_lo[at_row:]], axis=0)
            inv_v[b, at_row : at_row + 256, 0:256] = jnp.dot(left, right, preferred_element_type=F32)
            stores.append(
                load(inv_v.at[b, at_row : at_row + 256, 0:256], priv_h.at[b, at_row : at_row + 256])
            )
    for copy in (*stores, *store_shared):
        copy.wait()
    for copy in sent:
        copy.wait_send()


def on_device(private_seeds, private_inverse, coupling, shared_seed, shared_inverse):
    vmem = pltpu.VMEM
    priv, shared = pl.pallas_call(
        kernel,
        out_shape=(
            jax.ShapeDtypeStruct((2, 768, 256), F32),
            jax.ShapeDtypeStruct((16, 128, 256), F32),
        ),
        in_specs=[pl.BlockSpec(memory_space=pl.ANY)] * 5,
        out_specs=[pl.BlockSpec(memory_space=pl.ANY)] * 2,
        scratch_shapes=[
            vmem((2, 768, 256), F32),
            vmem((2, 768, 768), F32),
            vmem((2, 768, 2048), BF16),
            vmem((128, 256), F32),
            vmem((13312, 128), F32),
            vmem((2, 8, 2, 4, 96, 128), F32),
            vmem((4, 2, 8, 2, 32, 128), F32),
            *[vmem((2048, 256), BF16)] * 6,
            *[vmem((512, 1024), BF16)] * 2,
            vmem((2, 768, 768), BF16),
            vmem((2, 768, 768), BF16),
            vmem((256, 1536), BF16),
            vmem((2, 2, 2, 4, SY, 128), F32),
            vmem((2, 2, 2, 4, SZ, 128), F32),
            vmem((2, 2, 4, SY, 128), F32),
            vmem((2, 2, 4, SZ, 128), F32),
            vmem((2, 3, 2, SY, 128), F32),
            vmem((2, 3, SZ, 128), F32),
            vmem((2, SY, 128), F32),
            vmem((2, 4, SZ, 128), F32),
            vmem((2, 128, 256), F32),
            vmem((768, 256), BF16),
            vmem((4, 2, 128, 256), F32),
            vmem((2048, 256), BF16),
            *[vmem((126 * 32, 128), F32)] * 3,
            vmem((30 * 32, 128), F32),
            vmem((16, 2, 128, 128), F32),
            vmem((1024, 256), BF16),
            pltpu.SemaphoreType.DMA((16,)),
            pltpu.SemaphoreType.DMA((MESSAGES,)),
            pltpu.SemaphoreType.DMA((MESSAGES,)),
        ],
        compiler_params=pltpu.CompilerParams(
            collective_id=0, has_side_effects=True, vmem_limit_bytes=67_043_328
        ),
        name="adjoint",
    )(
        private_seeds[0, 0],
        private_inverse[0, 0],
        coupling[0],
        shared_seed[0],
        shared_inverse.reshape(16, 2, 4, 128, 128),
    )
    return priv[None, None], shared.reshape(1, 2048, 256)


def solution(mesh):
    return jax.shard_map(
        on_device,
        mesh=mesh,
        in_specs=(
            P("scen", "col", None, None, None),
            P("scen", "col", None, None, None),
            P("scen", None, None, "col"),
            P("col", "scen", None),
            P(None, None, None, "col", "scen"),
        ),
        out_specs=(P("scen", "col", None, None, None), P("col", None, None)),
        check_vma=False,
    )
```

```python
import jax
import jax.numpy as jnp
from jax import lax
from jax.experimental import pallas as pl
from jax.experimental.pallas import tpu as pltpu
from jax.sharding import PartitionSpec as P

MESH = pl.DeviceIdType.MESH
F32, BF16 = jnp.float32, jnp.bfloat16
ROWS = (32, 32, 32, 32)
START = (0, 32, 64, 96)
ORDER = ((0, 2, 1), (1, 2, 0), (2, 1, 0), (0, 1, 2))
SY, SZ = 80, 48
MESSAGES = 256


def split(value):
    high = value.astype(BF16)
    return high, (value - high.astype(F32)).astype(BF16)


def kernel(
    seeds_h, inv_h, coup_h, sseed_h, sinv_h,
    priv_h, shared_h,
    seeds_v, inv_v, coup_v, sseed_v, part, mland, mx, mh0, mh1, mh2, ml0, ml1, ml2, mxh, mxl,
    inv_hi, inv_lo, half_t, sy, sz, cy, cz, ly, lz, py, pz, rbuf, rcat, rx, rxcat, lr0, lr1, lr2, lr3, yg, yh,
    local_sem, send_sem, recv_sem,
):
    mhi, mlo, lands = (mh0, mh1, mh2), (ml0, ml1, ml2), (lr0, lr1, lr2, lr3)
    scen, col = lax.axis_index("scen"), lax.axis_index("col")
    core = lax.rem(scen, 2)
    y = lax.rem(lax.div(scen, 2), 4)
    zl = lax.div(scen, 8)
    x, zh = lax.rem(col, 4), lax.div(col, 4)
    z = zh * 2 + zl

    def device(x, y, z, core):
        return (lax.rem(z, 2) * 8 + y * 2 + core, lax.div(z, 2) * 4 + x)

    def ring(at, step):
        return lax.rem(at + step, 4)

    partner = device(x, y, z, 1 - core)
    zpair = ((1 - zl) * 8 + y * 2 + core, col)
    around = (
        (device(ring(x, 1), y, z, core), device(ring(x, 3), y, z, core)),
        (device(x, ring(y, 1), z, core), device(x, ring(y, 3), z, core)),
        (device(x, y, ring(z, 1), core), device(x, y, ring(z, 3), core)),
    )
    across = (device(ring(x, 2), y, z, core), device(x, ring(y, 2), z, core), device(x, y, ring(z, 2), core))
    crossed = [device(ring(x, step), y, z, 1 - core) for step in (2, 1, 3)]
    place = (x, y, z)

    loads = []

    def load(src, dst):
        copy = pltpu.make_async_copy(src, dst, local_sem.at[len(loads)])
        copy.start()
        loads.append(copy)
        return copy

    load_seeds = load(seeds_h, seeds_v)
    load_inv = [load(inv_h.at[b], inv_v.at[b]) for b in range(2)]
    load_coup = [load(coup_h.at[b], coup_v.at[b]) for b in range(2)]
    load_sseed = load(sseed_h, sseed_v)
    own_t, other_t = core * 8, (1 - core) * 8
    load_mx = load(sinv_h.at[pl.ds(own_t, 8), :, x, 96:128], mx.at[x, core])
    load_sinv = load(sinv_h.at[pl.ds(own_t, 8), :, :, 0:96], mland.at[core])

    barrier = pltpu.get_barrier_semaphore()
    for to in (partner, *around[0], *around[1], *around[2], *across, *crossed):
        pl.semaphore_signal(barrier, inc=1, device_id=to, device_id_type=MESH)
    pl.semaphore_wait(barrier, 13)

    sent = []

    def send(src, dst, to):
        copy = pltpu.make_async_remote_copy(
            src_ref=src,
            dst_ref=dst,
            send_sem=send_sem.at[len(sent)],
            recv_sem=recv_sem.at[len(sent)],
            device_id=to,
            device_id_type=MESH,
        )
        copy.start()
        sent.append(copy)
        return copy

    exchanged = []
    for step in (2, 1, 3):
        x_to = ring(x, step)
        for row, to_core in ((own_t, core), (other_t, 1 - core)):
            src = sinv_h.at[pl.ds(row, 8), :, x_to, 96:128]
            exchanged.append(send(src, mx.at[x, core], device(x_to, y, z, to_core)))
    exchanged.append(send(sinv_h.at[pl.ds(other_t, 8), :, x, 96:128], mx.at[x, core], partner))

    def swap_shared(half):
        return send(
            sinv_h.at[pl.ds(other_t + half * 4, 4), :, :, 0:96], mland.at[core, half * 4 : half * 4 + 4], partner
        )

    load_seeds.wait()
    for b in range(2):
        load_inv[b].wait()
        turned_hi, turned_lo = split(seeds_v[b].T)
        hi, lo = split(inv_v[b])
        inv_hi[b] = hi
        inv_lo[b] = lo
        for tile in range(3):
            depth, at = 256 * (tile + 1), 256 * tile
            left = jnp.concatenate(
                [turned_hi[:, :depth], turned_hi[:, :depth], turned_lo[:, :depth]], axis=1
            )
            right = jnp.concatenate(
                [
                    inv_hi[b, :depth, at : at + 256],
                    inv_lo[b, :depth, at : at + 256],
                    inv_hi[b, :depth, at : at + 256],
                ],
                axis=0,
            )
            first = jnp.dot(left, right, preferred_element_type=F32)
            half_t[:, b * 768 + at : b * 768 + at + 256] = first.astype(BF16)
            seeds_v[b, at : at + 256, :] = first.T

    for copy in load_coup:
        copy.wait()

    def seed_terms(zl_to):
        def body(y_to, carry):
            lane = pl.multiple_of((zl_to * 4 + y_to) * 256, 256)
            right = jnp.concatenate([coup_v[0, :, pl.ds(lane, 256)], coup_v[1, :, pl.ds(lane, 256)]], axis=0)
            out = jnp.dot(half_t[...], right, preferred_element_type=F32)
            for h in range(2):
                block = out[:, h * 128 : h * 128 + 128]
                for half in range(2):
                    sy[h, zl_to, half, y_to] = block[half * SY : half * SY + SY]
                    sz[h, zl_to, half, y_to] = block[2 * SY + half * SZ : 2 * SY + half * SZ + SZ]
            return carry

        lax.fori_loop(0, 4, body, 0)

    def add(to, *froms):
        total = to[...]
        for ref in froms:
            total = total + ref[...]
        to[...] = total

    def ring_start(view, land, axis):
        me, (plus, minus) = place[axis], around[axis]
        p1 = send(view(0, ring(me, 2)), land(0, 0), plus)
        m1 = send(view(1, ring(me, 2)), land(1, 0), minus)
        return [p1, m1]

    def ring_second(view, land, axis):
        me, (plus, minus) = place[axis], around[axis]
        p2 = send(view(1, ring(me, 1)), land(0, 1), plus)
        m2 = send(view(0, ring(me, 3)), land(1, 1), minus)
        return [p2, m2]

    def ring_third(view, land, axis, first):
        me, (plus, minus) = place[axis], around[axis]
        first[0].wait_recv()
        add(view(0, ring(me, 1)), land(0, 0))
        p3 = send(view(0, ring(me, 1)), land(0, 2), plus)
        first[1].wait_recv()
        add(view(1, ring(me, 3)), land(1, 0))
        m3 = send(view(1, ring(me, 3)), land(1, 2), minus)
        return [p3, m3]

    def ring_own(second, third):
        for copy in (*second, *third):
            copy.wait_recv()

    away = 1 - zl
    core_y, core_z = [], []
    for zl_to in (away, zl):
        seed_terms(zl_to)
        core_z.append(send(sz.at[1 - core, zl_to], cz.at[zl_to], partner))
        core_y.append(send(sy.at[1 - core, zl_to], cy.at[zl_to], partner))
    swaps = [swap_shared(half) for half in range(2)]

    def view_y(half, d):
        return sy.at[core, :, half, d]

    def view_z(half, d):
        return sz.at[core, zl, half, d]

    def land_y(way, message):
        return ly.at[way, message]

    def land_z(way, message):
        return lz.at[way, message]

    def split_shared(first, count):
        def body(block, carry):
            t, shard = lax.div(block, 8), lax.rem(block, 8)
            y_to, z_to, x_to = lax.rem(t, 4), lax.div(shard, 4) * 2 + lax.div(t, 4), lax.rem(shard, 4)
            near = mland[0, t, lax.div(shard, 4), x_to]
            far = mland[1, t, lax.div(shard, 4), x_to]
            hi, lo = split(jnp.concatenate([near, far], axis=1))
            to = (x_to, y_to, z_to)
            for colour in range(3):
                rows, start = ROWS[colour], START[colour]
                i, j, k = ORDER[colour]
                spot = pl.multiple_of(((to[i] * 4 + to[j]) * 4 + to[k]) * rows, rows)
                mhi[colour][pl.ds(spot, rows), :] = hi[start : start + rows]
                mlo[colour][pl.ds(spot, rows), :] = lo[start : start + rows]
            return carry

        lax.fori_loop(first, first + count, body, 0)

    core_z[0].wait_recv()
    add(sz.at[core, away], cz.at[away])
    pair_z = send(sz.at[core, away], pz, zpair)
    core_y[0].wait_recv()
    add(sy.at[core, away], cy.at[away])
    core_z[1].wait_recv()
    core_y[1].wait_recv()
    add(sy.at[core, zl], cy.at[zl])
    y_first = ring_start(view_y, land_y, 1)
    y_second = ring_second(view_y, land_y, 1)
    add(sz.at[core, zl], cz.at[zl])
    y_third = ring_third(view_y, land_y, 1, y_first)
    pair_z.wait_recv()
    add(sz.at[core, zl], pz)
    z_first = ring_start(view_z, land_z, 1)
    z_second = ring_second(view_z, land_z, 1)
    load_sinv.wait()
    swaps[0].wait_recv()
    split_shared(0, 32)
    ring_own(y_second, y_third)
    add(view_y(0, y), land_y(1, 1), land_y(0, 2))
    add(view_y(1, y), land_y(0, 1), land_y(1, 2))
    pair_y = [send(sy.at[core, away, half, y], py.at[half], zpair) for half in range(2)]
    z_third = ring_third(view_z, land_z, 1, z_first)
    swaps[1].wait_recv()
    split_shared(32, 32)
    pieces = []
    for half in range(2):
        pair_y[half].wait_recv()
        pieces.append(sy[core, zl, half, y] + py[half])
    ring_own(z_second, z_third)
    pieces.append(view_z(0, y)[...] + land_z(1, 1)[...] + land_z(0, 2)[...])
    pieces.append(view_z(1, y)[...] + land_z(0, 1)[...] + land_z(1, 2)[...])
    load_sseed.wait()
    rbuf[core] = sseed_v[...] - jnp.concatenate(pieces, axis=0).T
    swap_r = send(rbuf.at[core], rbuf.at[core], partner)
    gather_r = [
        send(rbuf.at[core], rx.at[x, core], to) for to in (across[0], *around[0])
    ]
    swap_r.wait_recv()
    r_hi, r_lo = split(jnp.concatenate([rbuf[0], rbuf[1]], axis=0))
    rcat[0:256] = r_hi
    rcat[256:512] = r_hi
    rcat[512:768] = r_lo

    def terms(colour, d):
        rows = ROWS[colour]
        base = 128 * START[colour]

        def body(j, carry):
            row = pl.multiple_of((d * 4 + j) * 4 * rows, 4 * rows)
            high = mhi[colour][pl.ds(row, 4 * rows), :]
            left = jnp.concatenate([high, mlo[colour][pl.ds(row, 4 * rows), :], high], axis=1)
            out = jnp.dot(left, rcat[...], preferred_element_type=F32)
            part[pl.ds(pl.multiple_of(base + row, rows), 4 * rows), :] = out[:, :128]
            part[pl.ds(pl.multiple_of(base + 64 * rows + row, rows), 4 * rows), :] = out[:, 128:]
            return carry

        lax.fori_loop(0, 4, body, 0)

    def views(colour, stage):
        rows = ROWS[colour]
        axes = ORDER[colour]
        size = (16, 4, 1)[stage] * rows
        half_size = (16 if colour == 3 else 64) * rows
        base = 128 * START[colour]
        for step in range(colour == 3, stage):
            base = base + place[axes[step]] * ((16, 4)[step] * rows)

        def view(half, d):
            return part.at[pl.ds(pl.multiple_of(base + half * half_size + d * size, 16), size)]

        span = (5 if colour == 3 else 21) * rows
        shift = ((0, 0, 4) if colour == 3 else (0, 16, 20))[stage] * rows

        def land(way, message):
            return lands[colour].at[pl.ds((way * 3 + message) * span + shift, size)]

        return view, land, axes[stage]

    def piece(ref, at_row, rows):
        return ref.at[pl.ds(pl.multiple_of(at_row, 16), rows)]

    def quarters(colour, stage):
        rows = (4, 1)[stage] * ROWS[colour]
        me = place[ORDER[colour][stage + 1]]
        return [(ring(me, step) * rows, rows) for step in (2, 1, 3, 0)]

    first, second, third, last = {}, {}, {}, {}

    def pass_sums(colour, stage):
        view, land, axis = views(colour, stage)
        me, (plus, minus) = place[axis], around[axis]
        third[colour] = []
        for way in range(2):
            first[colour][way].wait_recv()
        for at_row, rows in quarters(colour, stage):
            for way, to in ((0, plus), (1, minus)):
                out = piece(view(way, ring(me, 3 if way else 1)), at_row, rows)
                add(out, piece(land(way, 0), at_row, rows))
                third[colour].append(send(out, piece(land(way, 2), at_row, rows), to))

    def own_sums(colour, stage, step):
        view, land, axis = views(colour, stage)
        me = place[axis]
        if step == 0:
            for copy in second[colour]:
                copy.wait_recv()
            ready[colour] = []
            last[colour] = []
        at_row, rows = quarters(colour, stage)[step]
        for way in range(2):
            third[colour][2 * step + way].wait_recv()
        for half in range(2):
            add(
                piece(view(half, me), at_row, rows),
                piece(land(1 - half, 1), at_row, rows),
                piece(land(half, 2), at_row, rows),
            )
        view, land, axis = views(colour, stage + 1)
        me, (plus, minus) = place[axis], around[axis]
        if stage == 1:
            if step < 3:
                to = (across[axis], plus, minus)[step]
                for half in range(2):
                    last[colour].append(send(view(half, ring(me, (2, 1, 3)[step])), land(half, step), to))
        elif step == 0:
            ready[colour] = ring_start(view, land, axis)
        elif step == 1:
            ready[colour].append(send(view(1, ring(me, 1)), land(0, 1), plus))
        elif step == 2:
            ready[colour].append(send(view(0, ring(me, 3)), land(1, 1), minus))
        else:
            first[colour], second[colour] = ready[colour][:2], ready[colour][2:]

    yp, ym = around[1]
    back, ahead, opposite = ring(y, 3), ring(y, 1), ring(y, 2)
    block = core * 8 + zl * 4 + y

    def pass_on(ref, to):
        return send(ref, ref, to)

    def gather(start, rows, near, far):
        def at(zl_of, y_of, half, part_of=None):
            first_row, count = start, rows
            if part_of is not None:
                first_row, count = start + part_of * (rows // 2), rows // 2
            return yg.at[core * 8 + zl_of * 4 + y_of, half, first_row : first_row + count]

        y1 = [pass_on(at(zl, y, 1), yp), pass_on(at(zl, y, 1), ym)]
        z0 = pass_on(at(zl, y, 0), zpair)
        y0 = [pass_on(at(zl, y, 0), yp), pass_on(at(zl, y, 0), ym)]
        z1 = [pass_on(at(zl, y, 1), zpair)]
        for half in range(2):
            near.append(pass_on(at(zl, y, half), partner))
        yield
        y1[0].wait_recv()
        y1f = [pass_on(at(zl, back, 1, 0), yp)]
        z1.append(pass_on(at(zl, back, 1), zpair))
        y1[1].wait_recv()
        y1f.append(pass_on(at(zl, ahead, 1, 1), ym))
        z1.append(pass_on(at(zl, ahead, 1), zpair))
        z0.wait_recv()
        y0z = [pass_on(at(away, y, 0), yp), pass_on(at(away, y, 0), ym)]
        y0[0].wait_recv()
        y0f = [pass_on(at(zl, back, 0, 0), yp)]
        y0[1].wait_recv()
        y0f.append(pass_on(at(zl, ahead, 0, 1), ym))
        for half in (1, 0):
            near.append(pass_on(at(zl, back, half), partner))
            near.append(pass_on(at(zl, ahead, half), partner))
        far.append(pass_on(at(away, y, 0), partner))
        yield
        for copy in y1f:
            copy.wait_recv()
        z1.append(pass_on(at(zl, opposite, 1), zpair))
        near.append(pass_on(at(zl, opposite, 1), partner))
        y0z[0].wait_recv()
        y0zf = [pass_on(at(away, back, 0, 0), yp)]
        y0z[1].wait_recv()
        y0zf.append(pass_on(at(away, ahead, 0, 1), ym))
        for copy in y0f:
            copy.wait_recv()
        near.append(pass_on(at(zl, opposite, 0), partner))
        far.append(pass_on(at(away, back, 0), partner))
        far.append(pass_on(at(away, ahead, 0), partner))
        yield
        for copy, y_of in zip(z1, (y, back, ahead, opposite)):
            copy.wait_recv()
            far.append(pass_on(at(away, y_of, 1), partner))
        for copy in y0zf:
            copy.wait_recv()
        far.append(pass_on(at(away, opposite, 0), partner))

    def total_sums(colour):
        view, land, axis = views(colour, 2)
        for copy in last[colour]:
            copy.wait_recv()
        start, rows = START[colour], ROWS[colour]
        for half in range(2):
            total = view(half, place[axis])[...]
            for step in range(3):
                total = total + land(half, step)[...]
            yg[block, half, start : start + rows] = total

    ready = {}
    for colour in (1, 2, 0):
        view, land, axis = views(colour, 0)
        terms(colour, ring(place[axis], 2))
        first[colour] = ring_start(view, land, axis)
    for colour in (1, 2, 0):
        view, land, axis = views(colour, 0)
        terms(colour, ring(place[axis], 1))
        terms(colour, ring(place[axis], 3))
        second[colour] = ring_second(view, land, axis)
    for colour in (1, 2, 0):
        terms(colour, place[ORDER[colour][0]])
    load_mx.wait()
    for copy in exchanged:
        copy.wait_recv()

    def split_exchanged(block, carry):
        t, zh_of = lax.div(block, 2), lax.rem(block, 2)
        hi, lo = split(jnp.concatenate([mx[i, j, t, zh_of] for i in range(4) for j in range(2)], axis=1))
        row = pl.multiple_of((lax.rem(t, 4) * 4 + zh_of * 2 + lax.div(t, 4)) * 32, 32)
        mxh[pl.ds(row, 32), :] = hi
        mxl[pl.ds(row, 32), :] = lo
        return carry

    lax.fori_loop(0, 16, split_exchanged, 0)
    pass_sums(1, 0)
    pass_sums(2, 0)
    relayed = []
    for copy, step in zip(gather_r, (2, 3, 1)):
        copy.wait_recv()
        spot = rx.at[ring(x, step), core]
        relayed.append(send(spot, spot, partner))
    rx[x] = rbuf[...]
    for copy in relayed:
        copy.wait_recv()
    for i in range(8):
        hi, lo = split(rx[i // 2, i % 2])
        rxcat[i * 128 : i * 128 + 128] = hi
        rxcat[1024 + i * 128 : 1152 + i * 128] = lo

    def exchanged_terms(j, carry):
        row = pl.multiple_of(j * 128, 128)
        high, low = mxh[pl.ds(row, 128), :], mxl[pl.ds(row, 128), :]
        out = jnp.dot(high, rxcat[0:1024], preferred_element_type=F32)
        out += jnp.dot(low, rxcat[0:1024], preferred_element_type=F32)
        out += jnp.dot(high, rxcat[1024:2048], preferred_element_type=F32)
        part[pl.ds(pl.multiple_of(12288 + row, 128), 128), :] = out[:, :128]
        part[pl.ds(pl.multiple_of(12800 + row, 128), 128), :] = out[:, 128:]
        return carry

    lax.fori_loop(0, 4, exchanged_terms, 0)
    view, land, axis = views(3, 1)
    first[3] = ring_start(view, land, axis)
    second[3] = ring_second(view, land, axis)
    pass_sums(0, 0)
    for step in range(4):
        own_sums(1, 0, step)
        own_sums(2, 0, step)
    pass_sums(1, 1)
    pass_sums(2, 1)
    pass_sums(3, 1)
    for step in range(4):
        own_sums(0, 0, step)
    for step in range(4):
        for colour in (1, 2):
            own_sums(colour, 1, step)
    near, far = [], []
    early = gather(32, 96, near, far)
    late = gather(0, 32, near, far)
    pass_sums(0, 1)
    for step in range(4):
        own_sums(3, 1, step)
    for step in range(4):
        own_sums(0, 1, step)
    for colour in (1, 2, 3):
        total_sums(colour)
    next(early)
    total_sums(0)
    next(late)
    next(early)
    next(late)
    next(early)
    next(late)
    for _ in early:
        pass

    def subtract_coupled(zl_of):
        def round_block(i, carry):
            t = lax.div(i, 4) * 8 + zl_of * 4 + lax.rem(i, 4)
            row = pl.multiple_of(i * 128, 128)
            yh[pl.ds(row, 128), :] = jnp.concatenate([yg[t, 0], yg[t, 1]], axis=1).astype(BF16)
            return carry

        lax.fori_loop(0, 8, round_block, 0)
        lane = pl.multiple_of(zl_of * 512, 512)

        def body(tile, carry):
            row = pl.multiple_of(lax.rem(tile, 3) * 256, 256)
            b = lax.div(tile, 3)
            left = jnp.concatenate(
                [coup_v[b, pl.ds(row, 256), pl.ds(lane, 512)], coup_v[b, pl.ds(row, 256), pl.ds(lane + 1024, 512)]],
                axis=1,
            )
            seeds_v[b, pl.ds(row, 256), :] -= jnp.dot(left, yh[...], preferred_element_type=F32)
            return carry

        lax.fori_loop(0, 6, body, 0)

    def store_half(zl_of):
        return [
            load(
                yg.at[pl.ds(h * 8 + zl_of * 4, 4), half],
                shared_h.at[pl.ds(h * 8 + zl_of * 4, 4), :, half * 128 : half * 128 + 128],
            )
            for h in range(2)
            for half in range(2)
        ]

    for copy in near:
        copy.wait_recv()
    store_shared = store_half(zl)
    subtract_coupled(zl)
    for _ in late:
        pass
    for copy in far:
        copy.wait_recv()
    store_shared += store_half(away)
    subtract_coupled(away)

    stores = []
    for b in range(2):
        second_hi, second_lo = split(seeds_v[b])
        for tile in range(3):
            at_row = 256 * tile
            high = inv_hi[b, at_row : at_row + 256, at_row:]
            left = jnp.concatenate([high, inv_lo[b, at_row : at_row + 256, at_row:], high], axis=1)
            right = jnp.concatenate([second_hi[at_row:], second_hi[at_row:], second_lo[at_row:]], axis=0)
            inv_v[b, at_row : at_row + 256, 0:256] = jnp.dot(left, right, preferred_element_type=F32)
            stores.append(
                load(inv_v.at[b, at_row : at_row + 256, 0:256], priv_h.at[b, at_row : at_row + 256])
            )
    for copy in (*stores, *store_shared):
        copy.wait()
    for copy in sent:
        copy.wait_send()


def on_device(private_seeds, private_inverse, coupling, shared_seed, shared_inverse):
    vmem = pltpu.VMEM
    priv, shared = pl.pallas_call(
        kernel,
        out_shape=(
            jax.ShapeDtypeStruct((2, 768, 256), F32),
            jax.ShapeDtypeStruct((16, 128, 256), F32),
        ),
        in_specs=[pl.BlockSpec(memory_space=pl.ANY)] * 5,
        out_specs=[pl.BlockSpec(memory_space=pl.ANY)] * 2,
        scratch_shapes=[
            vmem((2, 768, 256), F32),
            vmem((2, 768, 768), F32),
            vmem((2, 768, 2048), BF16),
            vmem((128, 256), F32),
            vmem((13312, 128), F32),
            vmem((2, 8, 2, 4, 96, 128), F32),
            vmem((4, 2, 8, 2, 32, 128), F32),
            *[vmem((2048, 256), BF16)] * 6,
            *[vmem((512, 1024), BF16)] * 2,
            vmem((2, 768, 768), BF16),
            vmem((2, 768, 768), BF16),
            vmem((256, 1536), BF16),
            vmem((2, 2, 2, 4, SY, 128), F32),
            vmem((2, 2, 2, 4, SZ, 128), F32),
            vmem((2, 2, 4, SY, 128), F32),
            vmem((2, 2, 4, SZ, 128), F32),
            vmem((2, 3, 2, SY, 128), F32),
            vmem((2, 3, SZ, 128), F32),
            vmem((2, SY, 128), F32),
            vmem((2, 4, SZ, 128), F32),
            vmem((2, 128, 256), F32),
            vmem((768, 256), BF16),
            vmem((4, 2, 128, 256), F32),
            vmem((2048, 256), BF16),
            *[vmem((126 * 32, 128), F32)] * 3,
            vmem((30 * 32, 128), F32),
            vmem((16, 2, 128, 128), F32),
            vmem((1024, 256), BF16),
            pltpu.SemaphoreType.DMA((24,)),
            pltpu.SemaphoreType.DMA((MESSAGES,)),
            pltpu.SemaphoreType.DMA((MESSAGES,)),
        ],
        compiler_params=pltpu.CompilerParams(
            collective_id=0, has_side_effects=True, vmem_limit_bytes=67_043_328
        ),
        name="adjoint",
    )(
        private_seeds[0, 0],
        private_inverse[0, 0],
        coupling[0],
        shared_seed[0],
        shared_inverse.reshape(16, 2, 4, 128, 128),
    )
    return priv[None, None], shared.reshape(1, 2048, 256)


def solution(mesh):
    return jax.shard_map(
        on_device,
        mesh=mesh,
        in_specs=(
            P("scen", "col", None, None, None),
            P("scen", "col", None, None, None),
            P("scen", None, None, "col"),
            P("col", "scen", None),
            P(None, None, None, "col", "scen"),
        ),
        out_specs=(P("scen", "col", None, None, None), P("col", None, None)),
        check_vma=False,
    )
```
